512 devices in a mesh: block: 32 (over z, x), tile: 16 (over y, core).
Axes of the slice: x: 4, y: 8, z: 8, core: 2. Of those that a mesh axis runs over, the one named last changes fastest.
Arguments:
- params: float32 [59, 262144], P(None, ('block', 'tile')), may hold values from -4 to 3, as said below
- moment1: float32 [59, 262144], P(None, ('block', 'tile')), may hold values from -0.6 to 0.6
- moment2: float32 [59, 262144], P(None, ('block', 'tile')), may hold values from 0.01 to 1
- tile_lists: int32 [512, 8, 256], P(('block', 'tile')), may hold values from -1 to 8191, as said below
- cameras: float32 [32, 2, 8], P('block'), may hold values from -0.4 to 170, as said below
- targets: float32 [512, 8, 3, 256], P(('block', 'tile')), may hold values from 0 to 1
- boundary_index: int32 [512, 2, 128], P(('block', 'tile')), may hold values from 0 to 511, as said below
- links: int32 [32], replicated, may hold values 0 or 1
- consensus: float32 [512, 2, 59, 128], P(('block', 'tile')), may hold values from -6 to 6
- duals: float32 [512, 2, 59, 128], P(('block', 'tile')), may hold values from -0.6 to 0.6
Outputs:
- params_out: float32 [59, 262144], P(None, ('block', 'tile'))
- moment1_out: float32 [59, 262144], P(None, ('block', 'tile'))
- moment2_out: float32 [59, 262144], P(None, ('block', 'tile'))
- consensus_out: float32 [512, 2, 59, 128], P(('block', 'tile'))
- duals_out: float32 [512, 2, 59, 128], P(('block', 'tile'))
The draws below stay inside these ranges and needn't reach their ends.
Inputs may be any that keep to these rules, and one draw needn't show every extreme that they name: `params`: rows 0-2 lie in -1 to 1, rows 3-5 in -1 to 0, row 6 in 0.6 to 1.2, rows 7-9 in -1 to 1, row 10 in -4 to -1.5, rows 11 to 58 in -3 to 3. `cameras`: entries 0-3 are a quaternion whose first entry is 1 and others within -0.4 to 0.4, entries 4-5 lie in -0.3 to 0.3, entry 6 in 3.5 to 4.5, entry 7 in 130 to 170. `tile_lists`: -1 marks an empty slot; all empty slots of a list come after its live ones, and live entries stand in compositing order, front first. At most 16 live entries of one list are held by any one tile device, and in every list exactly 16 are held by some tile device. `boundary_index`: the 256 entries of one device are distinct. Entry [., 1, j] of device (b, t) and entry [., 0, j] of device (b + 1, t) are copies of one splat.
All inputs are finite; a program needn't handle non-finite values.
Results may differ from the reference program's by a relative error of at most 0.0003.
Values sent between devices are 32-bit elements; how exact they have to be, the bound alone decides.
No kernel may reach another device: no remote copies, remote signals or barrier semaphores. Data moves between devices by JAX's collectives and lax.ppermute only.
A program may use at most 64 MiB of HBM per device.

```python
import math
import jax
import jax.numpy as jnp
from jax import lax

PARAMS = 59
SPL_DEV = 512
CAP = 16
SCREENS = 4
NB = 128
VIEWS = 2
ROUNDS = 2
PIX = 256
BLOCKS = 32
LISTS = 8
KLIST = 256
NSPLAT = 262144
N_BLOCK = 32
N_TILE = 16
DEVICES = 512


def draw_params(key, part):
    keys = jax.random.split(jax.random.fold_in(key, 5), 7)
    count = NSPLAT
    centres = jax.random.uniform(keys[0], (3, count), jnp.float32, -1.0, 1.0)
    log_scales = jax.random.uniform(keys[1], (3, count), jnp.float32, -1.0, 0.0)
    quat_real = jax.random.uniform(keys[2], (1, count), jnp.float32, 0.6, 1.2)
    quat_rest = jnp.clip(0.4 * jax.random.normal(keys[3], (3, count), jnp.float32), -1.0, 1.0)
    opacity = jax.random.uniform(keys[4], (1, count), jnp.float32, -4.0, -1.5)
    sh_base = jnp.clip(0.5 * jax.random.normal(keys[5], (3, count), jnp.float32), -2.0, 2.0)
    sh_rest = 0.25 * jax.random.normal(keys[6], (45, count), jnp.float32)
    sh_rest = jnp.clip(sh_rest, -3.0, 3.0)
    sh_base = jnp.clip(sh_base, -3.0, 3.0)
    return jnp.concatenate([centres, log_scales, quat_real, quat_rest, opacity, sh_base, sh_rest], axis=0).astype(jnp.float32)


def draw_cameras(key, part):
    keys = jax.random.split(jax.random.fold_in(key, 31), 4)
    lead = (BLOCKS, VIEWS)
    tilt_part = jnp.clip(0.15 * jax.random.normal(keys[0], lead + (3,), jnp.float32), -0.4, 0.4)
    offset_xy = jax.random.uniform(keys[1], lead + (2,), jnp.float32, -0.3, 0.3)
    offset_z = jax.random.uniform(keys[2], lead + (1,), jnp.float32, 3.5, 4.5)
    focal_len = jax.random.uniform(keys[3], lead + (1,), jnp.float32, 130.0, 170.0)
    return jnp.concatenate([jnp.ones(lead + (1,), jnp.float32), tilt_part, offset_xy, offset_z, focal_len], axis=2).astype(jnp.float32)


def draw_tile_lists(key, part):
    keys = jax.random.split(jax.random.fold_in(key, 11), 4)
    list_total = DEVICES * LISTS
    counts = jax.random.randint(keys[0], (list_total, N_TILE), 1, CAP + 1)
    full_owner = jax.random.randint(keys[1], (list_total,), 0, N_TILE)
    owner_ids = jnp.arange(N_TILE, dtype=jnp.int32)
    counts = jnp.where(owner_ids[None, :] == full_owner[:, None], CAP, counts)
    locals_drawn = jax.random.randint(keys[2], (list_total, N_TILE, CAP), 0, SPL_DEV)
    slot_ids = jnp.arange(CAP, dtype=jnp.int32)
    is_live = slot_ids[None, None, :] < counts[:, :, None]
    entries = jnp.where(is_live, owner_ids[None, :, None] * SPL_DEV + locals_drawn, -1).reshape(list_total, KLIST)
    jitter = jax.random.randint(keys[3], (list_total, KLIST), 0, 1 << 19)
    scores = jnp.where(entries >= 0, 0, 1 << 30) + jitter * KLIST + jnp.arange(KLIST, dtype=jnp.int32)[None, :]
    order = jnp.argsort(scores, axis=1)
    entries = jnp.take_along_axis(entries, order, axis=1)
    return entries.reshape(DEVICES, LISTS, KLIST).astype(jnp.int32)


def draw_boundary_index(key, part):
    keys = jax.random.split(jax.random.fold_in(key, 23), DEVICES)
    chosen = jax.vmap(lambda device_key: jax.random.permutation(device_key, SPL_DEV)[:2 * NB])(keys)
    return chosen.reshape(DEVICES, 2, NB).astype(jnp.int32)


def with_ends(values, own_key, smallest, high):
    extent = values.shape
    place = [jax.random.randint(jax.random.fold_in(own_key, axis), (), 0, extent[axis]) for axis in range(len(extent))]
    values = values.at[tuple(place)].set(smallest)
    longest = extent.index(max(extent))
    place[longest] = (place[longest] + 1) % extent[longest]
    return values.at[tuple(place)].set(high)


def steps_of(own_key, extent, cuts, least, high):
    level, own = 1.0, jax.random.fold_in(own_key, 6)
    for position, parts in cuts:
        heights = jnp.exp(jax.random.uniform(jax.random.fold_in(own, position), (parts,), jnp.float32, least / len(cuts), high / len(cuts)))
        level = level * jnp.repeat(heights, extent[position] // parts).reshape([-1 if axis == position else 1 for axis in range(len(extent))])
    return level


def normal_values(stream_key, extent, width, limit, cuts=(), kind=jnp.bfloat16):
    values = jax.random.normal(stream_key, extent, jnp.float32) * width
    if len(cuts) > 0:
        values = steps_of(stream_key, extent, cuts, -0.22, 0.18) * values
    return jnp.clip(values, min=-limit, max=limit).astype(kind)


def setup_inputs(seed: int = 0) -> dict:
    streams_of = jax.random.split(jax.random.key(seed), 11)
    return {
        "params": draw_params(jax.random.fold_in(streams_of[10], 71), 0),
        "moment1": normal_values(streams_of[1], (PARAMS, NSPLAT), 0.1, 0.6, ((1, 512),), jnp.float32),
        "moment2": jnp.clip(jnp.exp(math.log(1.0) - 4.6051702 * jax.random.uniform(streams_of[2], (PARAMS, NSPLAT), jnp.float32) ** steps_of(streams_of[2], (PARAMS, NSPLAT), ((1, 512),), -0.2, 0.2)), 0.01, 1.0),
        "tile_lists": draw_tile_lists(jax.random.fold_in(streams_of[10], 71), 0),
        "cameras": draw_cameras(jax.random.fold_in(streams_of[10], 71), 0),
        "targets": jnp.clip(1.0 * jax.random.uniform(streams_of[5], (DEVICES, LISTS, 3, PIX), jnp.float32) ** steps_of(streams_of[5], (DEVICES, LISTS, 3, PIX), ((0, 512),), -0.2, 0.2), 0.0, 1.0),
        "boundary_index": draw_boundary_index(jax.random.fold_in(streams_of[10], 71), 0),
        "links": with_ends((jax.random.randint(streams_of[7], (BLOCKS,), 0, 4) < 3).astype(jnp.int32), jax.random.fold_in(streams_of[7], 1), 0, 1),
        "consensus": normal_values(streams_of[8], (DEVICES, 2, PARAMS, NB), 1.0, 6.0, ((0, 512),), jnp.float32),
        "duals": normal_values(streams_of[9], (DEVICES, 2, PARAMS, NB), 0.1, 0.6, ((0, 512),), jnp.float32),
    }


sh_zero = 0.28209479177387814
sh_one = 0.4886025119029199
sh_two = (1.0925484305920792, -1.0925484305920792, 0.31539156525252005, -1.0925484305920792, 0.5462742152960396)
sh_three = (-0.5900435899266435, 2.890611442640554, -0.4570457994644658, 0.3731763325901154, -0.4570457994644658, 1.445305721320277, -0.5900435899266435)
beta_one = 0.9
beta_two = 0.999
learn_rate = 0.01
adam_eps = 1e-08
penalty = 2.0
first_step = 100
blur_var = 0.3
opacity_cap = 0.99
highest = lax.Precision.HIGHEST

def rotation(quat_w, quat_x, quat_y, quat_z):
    inverse = lax.rsqrt(quat_w * quat_w + quat_x * quat_x + quat_y * quat_y + quat_z * quat_z)
    unit_w = quat_w * inverse
    unit_x = quat_x * inverse
    unit_y = quat_y * inverse
    unit_z = quat_z * inverse
    return ((1.0 - 2.0 * (unit_y * unit_y + unit_z * unit_z), 2.0 * (unit_x * unit_y - unit_w * unit_z), 2.0 * (unit_x * unit_z + unit_w * unit_y)), (2.0 * (unit_x * unit_y + unit_w * unit_z), 1.0 - 2.0 * (unit_x * unit_x + unit_z * unit_z), 2.0 * (unit_y * unit_z - unit_w * unit_x)), (2.0 * (unit_x * unit_z - unit_w * unit_y), 2.0 * (unit_y * unit_z + unit_w * unit_x), 1.0 - 2.0 * (unit_x * unit_x + unit_y * unit_y)))

def sh_terms(dir_x, dir_y, dir_z):
    sq_x = dir_x * dir_x
    sq_y = dir_y * dir_y
    sq_z = dir_z * dir_z
    return (sh_zero + 0.0 * dir_x, -sh_one * dir_y, sh_one * dir_z, -sh_one * dir_x, sh_two[0] * dir_x * dir_y, sh_two[1] * dir_y * dir_z, sh_two[2] * (2.0 * sq_z - sq_x - sq_y), sh_two[3] * dir_x * dir_z, sh_two[4] * (sq_x - sq_y), sh_three[0] * dir_y * (3.0 * sq_x - sq_y), sh_three[1] * dir_x * dir_y * dir_z, sh_three[2] * dir_y * (4.0 * sq_z - sq_x - sq_y), sh_three[3] * dir_z * (2.0 * sq_z - 3.0 * sq_x - 3.0 * sq_y), sh_three[4] * dir_x * (4.0 * sq_z - sq_x - sq_y), sh_three[5] * dir_z * (sq_x - sq_y), sh_three[6] * dir_x * (sq_x - 3.0 * sq_y))

def render_list(splats, live_mask, camera, pixel_x, pixel_y, centre_y, goal_img):
    cam_rot = rotation(camera[0], camera[1], camera[2], camera[3])
    shift_vec = (camera[4], camera[5], camera[6])
    focal_len = camera[7]
    centre = (splats[0], splats[1], splats[2])
    in_cam = [cam_rot[row_idx][0] * centre[0] + cam_rot[row_idx][1] * centre[1] + cam_rot[row_idx][2] * centre[2] + shift_vec[row_idx] for row_idx in range(3)]
    inv_depth = 1.0 / in_cam[2]
    mean_x = focal_len * in_cam[0] * inv_depth + 64.0
    mean_y = focal_len * in_cam[1] * inv_depth + centre_y
    jacobian = ((focal_len * inv_depth, 0.0, -focal_len * in_cam[0] * inv_depth * inv_depth), (0.0, focal_len * inv_depth, -focal_len * in_cam[1] * inv_depth * inv_depth))
    screen_map = [[jacobian[row_idx][0] * cam_rot[0][col_idx] + jacobian[row_idx][1] * cam_rot[1][col_idx] + jacobian[row_idx][2] * cam_rot[2][col_idx] for col_idx in range(3)] for row_idx in range(2)]
    local_rot = rotation(splats[6], splats[7], splats[8], splats[9])
    scales = [jnp.exp(splats[3 + col_idx]) for col_idx in range(3)]
    axes_flat = [[(screen_map[row_idx][0] * local_rot[0][col_idx] + screen_map[row_idx][1] * local_rot[1][col_idx] + screen_map[row_idx][2] * local_rot[2][col_idx]) * scales[col_idx] for col_idx in range(3)] for row_idx in range(2)]
    cov_xx = axes_flat[0][0] * axes_flat[0][0] + axes_flat[0][1] * axes_flat[0][1] + axes_flat[0][2] * axes_flat[0][2] + blur_var
    cov_xy = axes_flat[0][0] * axes_flat[1][0] + axes_flat[0][1] * axes_flat[1][1] + axes_flat[0][2] * axes_flat[1][2]
    cov_yy = axes_flat[1][0] * axes_flat[1][0] + axes_flat[1][1] * axes_flat[1][1] + axes_flat[1][2] * axes_flat[1][2] + blur_var
    determinant = cov_xx * cov_yy - cov_xy * cov_xy
    prec_xx = cov_yy / determinant
    prec_xy = -cov_xy / determinant
    prec_yy = cov_xx / determinant
    off_x = pixel_x[:, None] - mean_x[None, :]
    off_y = pixel_y[:, None] - mean_y[None, :]
    quadric = prec_xx[None, :] * off_x * off_x + 2.0 * prec_xy[None, :] * off_x * off_y + prec_yy[None, :] * off_y * off_y
    opacity = opacity_cap * jax.nn.sigmoid(splats[10]) * live_mask
    alpha_val = opacity[None, :] * jnp.exp(-0.5 * quadric)
    log_keep = jnp.log1p(-alpha_val)
    weights = jnp.exp(jnp.cumsum(log_keep, axis=1) - log_keep) * alpha_val
    eye_pos = [-(cam_rot[0][col_idx] * shift_vec[0] + cam_rot[1][col_idx] * shift_vec[1] + cam_rot[2][col_idx] * shift_vec[2]) for col_idx in range(3)]
    view_dir = [centre[col_idx] - eye_pos[col_idx] for col_idx in range(3)]
    inverse = lax.rsqrt(view_dir[0] * view_dir[0] + view_dir[1] * view_dir[1] + view_dir[2] * view_dir[2])
    terms = sh_terms(view_dir[0] * inverse, view_dir[1] * inverse, view_dir[2] * inverse)
    colours = jnp.stack([sum((terms[term_idx] * splats[11 + 3 * term_idx + chan_idx] for term_idx in range(16))) + 0.5 for chan_idx in range(3)])
    picture = jnp.einsum('pk,ck->cp', weights, colours, precision=highest)
    return 0.5 * jnp.sum((picture - goal_img) * (picture - goal_img))

def render_all(splats, live_vals, cameras, observed, tile_idx, centre_y):
    list_count = splats.shape[0]
    screens = list_count // cameras.shape[0]
    pixel_ids = jnp.arange(PIX, dtype=jnp.int32)

    def render_one(packed):
        splat_cols, live_mask, goal_img, list_idx = packed
        camera = cameras[list_idx // screens]
        number = tile_idx * screens + list_idx % screens
        pixel_x = (16 * (number % 8) + pixel_ids % 16).astype(jnp.float32) + 0.5
        pixel_y = (16 * (number // 8) + pixel_ids // 16).astype(jnp.float32) + 0.5
        return render_list(splat_cols, live_mask, camera, pixel_x, pixel_y, centre_y, goal_img)
    losses = lax.map(jax.checkpoint(render_one), (splats, live_vals, observed, jnp.arange(list_count, dtype=jnp.int32)))
    return jnp.sum(losses)

def local_grad(splats, live_vals, cameras, observed, tile_idx, centre_y):

    def loss_of(inputs):
        return render_all(inputs, live_vals, cameras, observed, tile_idx, centre_y)
    loss_val, pullback = jax.vjp(loss_of, splats)
    return pullback(jnp.ones_like(loss_val))[0]

def adam_step(values, moment_one, moment_two, grads, step):
    moment_one = beta_one * moment_one + (1.0 - beta_one) * grads
    moment_two = beta_two * moment_two + (1.0 - beta_two) * grads * grads
    corr_one = 1.0 - beta_one ** step
    corr_two = 1.0 - beta_two ** step
    values = values - learn_rate * (moment_one / corr_one) / (jnp.sqrt(moment_two / corr_two) + adam_eps)
    return (values, moment_one, moment_two)

def reference(params, moment1, moment2, tile_lists, cameras, targets, boundary_index, links, consensus, duals):
    per_block = N_TILE * SPL_DEV
    list_count = VIEWS * SCREENS
    centre_y = 8.0 * (N_TILE * SCREENS // 8)

    def to_blocks(array):
        return array.reshape(PARAMS, N_BLOCK, per_block).transpose(1, 0, 2)

    def from_blocks(array):
        return array.transpose(1, 0, 2).reshape(PARAMS, N_BLOCK * per_block)

    def side_blocks(array):
        return array.reshape(N_BLOCK, N_TILE, 2, PARAMS, NB).transpose(0, 2, 3, 1, 4).reshape(N_BLOCK, 2, PARAMS, N_TILE * NB)

    def side_devices(array):
        return array.reshape(N_BLOCK, 2, PARAMS, N_TILE, NB).transpose(0, 3, 1, 2, 4).reshape(N_BLOCK * N_TILE, 2, PARAMS, NB)
    values = to_blocks(params)
    moment_one = to_blocks(moment1)
    moment_two = to_blocks(moment2)
    list_ids = tile_lists.reshape(N_BLOCK, N_TILE, list_count, KLIST)
    goals = targets.reshape(N_BLOCK, N_TILE, list_count, 3, PIX)
    offsets = jnp.arange(N_TILE, dtype=jnp.int32) * SPL_DEV
    side_ids = (boundary_index.reshape(N_BLOCK, N_TILE, 2, NB) + offsets[None, :, None, None]).transpose(0, 2, 1, 3).reshape(N_BLOCK, 2 * N_TILE * NB)
    agreed = side_blocks(consensus)
    dual_vars = side_blocks(duals)
    link_vals = links.astype(jnp.float32)
    block_ids = jnp.arange(N_BLOCK, dtype=jnp.int32)
    right_w = jnp.where(block_ids < N_BLOCK - 1, link_vals, 0.0)
    left_w = jnp.concatenate([jnp.zeros((1,), jnp.float32), link_vals[:-1]])
    side_w = jnp.stack([left_w, right_w], axis=1)[:, :, None, None]

    def gather_sides(state):
        picked = jax.vmap(lambda block_vals, side_list: jnp.take(block_vals, side_list, axis=1))(state, side_ids)
        return picked.reshape(N_BLOCK, PARAMS, 2, N_TILE * NB).transpose(0, 2, 1, 3)

    def block_grad(packed):
        block_vals, block_lists, block_cams, block_goals = packed

        def tile_step(summed, tile_pack):
            tile_list_ids, tile_goals, tile_idx = tile_pack
            live_mask = tile_list_ids >= 0
            safe_ids = jnp.where(live_mask, tile_list_ids, 0).reshape(-1)
            splats = jnp.take(block_vals, safe_ids, axis=1).reshape(PARAMS, list_count, KLIST).transpose(1, 0, 2)
            grads = local_grad(splats, live_mask.astype(jnp.float32), block_cams, tile_goals, tile_idx, centre_y)
            return (summed.at[:, safe_ids].add(grads.transpose(1, 0, 2).reshape(PARAMS, -1)), None)
        return lax.scan(tile_step, jnp.zeros((PARAMS, per_block), jnp.float32), (block_lists, block_goals, jnp.arange(N_TILE, dtype=jnp.int32)))[0]
    for round_idx in range(ROUNDS):
        grads = lax.map(block_grad, (values, list_ids, cameras, goals))
        own_sides = gather_sides(values)
        prox = penalty * side_w * (own_sides - agreed + dual_vars)
        prox_flat = prox.transpose(0, 2, 1, 3).reshape(N_BLOCK, PARAMS, 2 * N_TILE * NB)
        grads = jax.vmap(lambda grad_blk, side_list, prox_blk: grad_blk.at[:, side_list].add(prox_blk))(grads, side_ids, prox_flat)
        values, moment_one, moment_two = adam_step(values, moment_one, moment_two, grads, first_step + round_idx + 1)
        own_sides = gather_sides(values)
        shared = own_sides + dual_vars
        from_left = jnp.concatenate([jnp.zeros_like(shared[:1, 1]), shared[:-1, 1]], axis=0)
        from_right = jnp.concatenate([shared[1:, 0], jnp.zeros_like(shared[:1, 0])], axis=0)
        partner = jnp.stack([from_left, from_right], axis=1)
        agreed = side_w * (shared + partner) * 0.5 + (1.0 - side_w) * own_sides
        dual_vars = dual_vars + side_w * (own_sides - agreed)
    return (from_blocks(values), from_blocks(moment_one), from_blocks(moment_two), side_devices(agreed), side_devices(dual_vars))
```

```python
import functools
import jax
import jax.numpy as jnp
from jax import lax
from jax.experimental import pallas as pl
from jax.experimental.pallas import tpu as pltpu
from jax.sharding import PartitionSpec as P

PARAMS = 59
SCREENS = 4
ROUNDS = 2
LISTS = 8
CAP = 16
SLOTS = 256
TILES = 16
SPL = 512
NB = 128
ROWS = 16
FEATS = 9
WIDE = 72
TOGETHER = 2
GRANT = 10 << 20

sh_zero = 0.28209479177387814
sh_one = 0.4886025119029199
sh_two = (
    1.0925484305920792,
    -1.0925484305920792,
    0.31539156525252005,
    -1.0925484305920792,
    0.5462742152960396,
)
sh_three = (
    -0.5900435899266435,
    2.890611442640554,
    -0.4570457994644658,
    0.3731763325901154,
    -0.4570457994644658,
    1.445305721320277,
    -0.5900435899266435,
)
beta_one = 0.9
beta_two = 0.999
learn_rate = 0.01
adam_eps = 1e-08
penalty = 2.0
first_step = 100
blur_var = 0.3
opacity_cap = 0.99
log2e = 1.4426950408889634

f32 = jnp.float32
bf16 = jnp.bfloat16
i32 = jnp.int32
VMEM = pltpu.VMEM
ANY_VMEM = pl.BlockSpec(memory_space=pltpu.VMEM)
ANY_SMEM = pl.BlockSpec(memory_space=pltpu.SMEM)


def iota(shape, axis):
    return lax.broadcasted_iota(i32, shape, axis)


def dot(a, b):
    return lax.dot_general(a, b, (((1,), (0,)), ((), ())), preferred_element_type=f32)


def dot_t(a, b):
    return lax.dot_general(a, b, (((1,), (1,)), ((), ())), preferred_element_type=f32)


def split(value):
    high = value.astype(bf16)
    return high, (value - high.astype(f32)).astype(bf16)


def lane_gather(value, index):
    return jnp.take_along_axis(value, index, axis=1, mode="promise_in_bounds")


def rotation(quat_w, quat_x, quat_y, quat_z):
    inverse = lax.rsqrt(quat_w * quat_w + quat_x * quat_x + quat_y * quat_y + quat_z * quat_z)
    unit_w = quat_w * inverse
    unit_x = quat_x * inverse
    unit_y = quat_y * inverse
    unit_z = quat_z * inverse
    return (
        (
            1.0 - 2.0 * (unit_y * unit_y + unit_z * unit_z),
            2.0 * (unit_x * unit_y - unit_w * unit_z),
            2.0 * (unit_x * unit_z + unit_w * unit_y),
        ),
        (
            2.0 * (unit_x * unit_y + unit_w * unit_z),
            1.0 - 2.0 * (unit_x * unit_x + unit_z * unit_z),
            2.0 * (unit_y * unit_z - unit_w * unit_x),
        ),
        (
            2.0 * (unit_x * unit_z - unit_w * unit_y),
            2.0 * (unit_y * unit_z + unit_w * unit_x),
            1.0 - 2.0 * (unit_x * unit_x + unit_y * unit_y),
        ),
    )


def sh_terms(dir_x, dir_y, dir_z):
    sq_x = dir_x * dir_x
    sq_y = dir_y * dir_y
    sq_z = dir_z * dir_z
    return (
        -sh_one * dir_y,
        sh_one * dir_z,
        -sh_one * dir_x,
        sh_two[0] * dir_x * dir_y,
        sh_two[1] * dir_y * dir_z,
        sh_two[2] * (2.0 * sq_z - sq_x - sq_y),
        sh_two[3] * dir_x * dir_z,
        sh_two[4] * (sq_x - sq_y),
        sh_three[0] * dir_y * (3.0 * sq_x - sq_y),
        sh_three[1] * dir_x * dir_y * dir_z,
        sh_three[2] * dir_y * (4.0 * sq_z - sq_x - sq_y),
        sh_three[3] * dir_z * (2.0 * sq_z - 3.0 * sq_x - 3.0 * sq_y),
        sh_three[4] * dir_x * (4.0 * sq_z - sq_x - sq_y),
        sh_three[5] * dir_z * (sq_x - sq_y),
        sh_three[6] * dir_x * (sq_x - 3.0 * sq_y),
    )


def camera_of(cam_ref):
    first = iota((8, 128), 0) < 4
    vals = [jnp.where(first, cam_ref[0, 0, i], cam_ref[0, 1, i]) for i in range(8)]
    rot = rotation(vals[0], vals[1], vals[2], vals[3])
    shift = vals[4:7]
    eye = [-(rot[0][c] * shift[0] + rot[1][c] * shift[1] + rot[2][c] * shift[2]) for c in range(3)]
    return rot, shift, vals[7], eye


def geometry(centre, log_scales, quat, cam):
    cam_rot, shift, focal, _ = cam
    in_cam = [
        cam_rot[r][0] * centre[0] + cam_rot[r][1] * centre[1] + cam_rot[r][2] * centre[2] + shift[r]
        for r in range(3)
    ]
    inv_depth = 1.0 / in_cam[2]
    scaled = focal * inv_depth
    ratio_x = in_cam[0] * inv_depth
    ratio_y = in_cam[1] * inv_depth
    mean_x = focal * ratio_x
    mean_y = focal * ratio_y
    screen_map = [
        [scaled * (cam_rot[0][c] - ratio_x * cam_rot[2][c]) for c in range(3)],
        [scaled * (cam_rot[1][c] - ratio_y * cam_rot[2][c]) for c in range(3)],
    ]
    local_rot = rotation(*quat)
    scales = [jnp.exp(s) for s in log_scales]
    axes = [
        [
            (
                screen_map[r][0] * local_rot[0][c]
                + screen_map[r][1] * local_rot[1][c]
                + screen_map[r][2] * local_rot[2][c]
            )
            * scales[c]
            for c in range(3)
        ]
        for r in range(2)
    ]
    cov_xx = axes[0][0] * axes[0][0] + axes[0][1] * axes[0][1] + axes[0][2] * axes[0][2] + blur_var
    cov_xy = axes[0][0] * axes[1][0] + axes[0][1] * axes[1][1] + axes[0][2] * axes[1][2]
    cov_yy = axes[1][0] * axes[1][0] + axes[1][1] * axes[1][1] + axes[1][2] * axes[1][2] + blur_var
    return mean_x, mean_y, cov_xx, cov_xy, cov_yy


def colours_of(centre, coeffs, cam):
    eye = cam[3]
    view = [centre[c] - eye[c] for c in range(3)]
    inverse = lax.rsqrt(view[0] * view[0] + view[1] * view[1] + view[2] * view[2])
    terms = sh_terms(view[0] * inverse, view[1] * inverse, view[2] * inverse)
    out = []
    for ch in range(3):
        total = sh_zero * coeffs[ch] + 0.5
        for q in range(15):
            total = total + terms[q] * coeffs[3 * (q + 1) + ch]
        out.append(total)
    return out


def precision_of(cov_xx, cov_xy, cov_yy):
    inverse = 1.0 / (cov_xx * cov_yy - cov_xy * cov_xy)
    return cov_yy * inverse, -cov_xy * inverse, cov_xx * inverse


def spread(x_ref, wide):
    for a in range(0, PARAMS, 8):
        n = min(8, PARAMS - a)
        for k in range(4):
            piece = x_ref[a : a + n, 128 * k : 128 * (k + 1)]
            for v in range(2):
                wide[pl.ds(8 * a + 4 * v + k, n, stride=8), :] = piece


def wide_row(wide, i):
    return wide[8 * i : 8 * i + 8, :]


def make_features(wide, cam, centre_y, feat):
    centre = [wide_row(wide, i) for i in range(3)]
    geo = geometry(
        centre, [wide_row(wide, 3 + i) for i in range(3)], [wide_row(wide, 6 + i) for i in range(4)], cam
    )
    prec = precision_of(geo[2], geo[3], geo[4])
    cols = colours_of(centre, [wide_row(wide, 11 + i) for i in range(48)], cam)
    opac = opacity_cap * jax.nn.sigmoid(wide_row(wide, 10))
    values = (*cols, geo[0] + 64.0, geo[1] + centre_y, *prec, opac)
    for f in range(FEATS):
        feat[8 * f : 8 * f + 8, :] = values[f]


def pick_features(sources, opac, index_row):
    row = iota((8, 128), 0)
    first = iota((8, 128), 1) < 64
    index = jnp.broadcast_to(jnp.maximum(index_row, 0), (8, 128))
    low = index & 127
    part = index >> 7
    both = []
    for v in range(2):
        got = [lane_gather(sources[v][k], low) for k in range(4)]
        both.append(
            jnp.where(part < 2, jnp.where(part == 0, got[0], got[1]), jnp.where(part == 2, got[2], got[3]))
        )
    last = jnp.where(row == jnp.where(first, 0, 4) + part, lane_gather(opac, low), 0.0)
    return jnp.where(first, both[0], both[1]), jnp.sum(last, axis=0, keepdims=True)


def sources_of(load):
    return [[load(pl.ds(4 * v + k, 8, stride=8)) for k in range(4)] for v in range(2)]


def lists_kernel(lists_ref, bidx_ref, before_ref, live_ref, req_ref, inv_ref):
    sub = iota((SLOTS, SLOTS), 0)
    lane = iota((SLOTS, SLOTS), 1)
    upto = jnp.where(sub <= lane, 1.0, 0.0).astype(bf16)
    number = (iota((SLOTS, 128), 0) + 1).astype(f32).astype(bf16)
    slot = iota((1, SLOTS), 1)
    row8 = iota((8, SLOTS), 0)
    owners = iota((TILES, SLOTS), 0)
    row = iota((8, 128), 0)
    col = iota((8, 128), 1)
    pick = row * CAP + (col & (CAP - 1))
    acc = [jnp.full((8, 128), -1, i32) for _ in range(2)]
    for l in range(LISTS):
        ids = lists_ref[0, l : l + 1, :]
        live = ids >= 0
        owner = jnp.where(live, ids >> 9, -1)
        local = ids & (SPL - 1)
        mine = owner == owners
        counts = dot(jnp.where(mine, 1.0, 0.0).astype(bf16), upto)
        rank = jnp.sum(jnp.where(mine, counts, 0.0), axis=0, keepdims=True).astype(i32) - 1
        place = jnp.where(live, owner * CAP + rank, -1)
        chosen = jnp.where(place == sub, 1.0, 0.0).astype(bf16)
        rows = jnp.where(
            row8 == 0, slot + 1, jnp.where(row8 == 1, local & 255, jnp.where(row8 == 2, local >> 8, 0))
        )
        found = dot_t(rows.astype(f32).astype(bf16), chosen)
        order = found[0:1, :]
        column = dot(chosen, number)
        before_ref[l] = jnp.where(jnp.concatenate([column, column], axis=1) < order, 1.0, 0.0).astype(bf16)
        held = order > 0.5
        live_ref[l : l + 1, :] = jnp.where(held, 1.0, 0.0)
        wanted = jnp.where(held, found[1:2, :] + 256.0 * found[2:3, :], -1.0).astype(i32)
        for h in range(2):
            half = jnp.broadcast_to(wanted[:, 128 * h : 128 * (h + 1)], (8, 128))
            acc[h] = jnp.where((col >> 4) == l, lane_gather(half, pick), acc[h])
    for o in range(TILES):
        req_ref[o] = acc[o // 8][o % 8 : o % 8 + 1, :]
    total = jnp.zeros((8, SPL), f32)
    sub_n = iota((SPL, NB), 0)
    for e in range(2):
        hit = jnp.where(bidx_ref[0, e : e + 1, :] == sub_n, 1.0, 0.0).astype(bf16)
        total = total + dot_t((col + (NB * e + 1)).astype(f32).astype(bf16), hit)
    inv_ref[...] = total.astype(i32) - 1


def features_kernel(centre_y, x_ref, cam_ref, feat_ref, wide):
    spread(x_ref, wide)
    make_features(wide, camera_of(cam_ref), centre_y, feat_ref)


def render_kernel(
    first_round,
    tile_ref,
    msg_in,
    before_ref,
    live_ref,
    goal_ref,
    *rest,
):
    if first_round:
        req_ref, out_ref, msg_ref = rest[0], rest[1], rest[-1]
        rest = rest[2:-1]
        for o in range(TILES):
            main, last = pick_features(
                sources_of(lambda rows: msg_in[o, rows, :]), msg_in[o, 64:72, :], req_ref[o]
            )
            msg_ref[o, 0:8, :] = main
            msg_ref[o, 8:9, :] = last
            out_ref[o, 9:10, :] = req_ref[o].astype(f32)
    else:
        msg_ref, out_ref = msg_in, rest[0]
        rest = rest[1:]
    feat, grad, grad8, goal8, alpha, lk_h, lk_l, wgt, wgt_h, wgt_l, u_f, u_h, u_l = rest
    row = iota((8, 128), 0)
    col = iota((8, 128), 1)
    block = col >> 4
    inner = col & (CAP - 1)
    for h in range(2):
        whole = [msg_ref[8 * h + o, 0:8, :] for o in range(8)]
        ninth = jnp.concatenate([msg_ref[8 * h + o, 8:9, :] for o in range(8)], axis=0)
        for l in range(LISTS):
            got = whole[l]
            for o in range(8):
                if o != l:
                    got = jnp.where(block == o, pltpu.roll(whole[o], (o - l) * CAP % 128, 1), got)
            feat[l, 0:8, 128 * h : 128 * (h + 1)] = got
            last = jnp.where(row == block, lane_gather(ninth, inner + CAP * l), 0.0)
            feat[l, 8:9, 128 * h : 128 * (h + 1)] = jnp.sum(last, axis=0, keepdims=True)
    goal8[...] = jnp.zeros_like(goal8)
    tile = tile_ref[0]
    sub16 = iota((16, SLOTS), 0).astype(f32)
    row8 = iota((8, SLOTS), 0)
    half = -0.5 * log2e
    group = range(TOGETHER)
    down = functools.partial(jnp.sum, axis=0, keepdims=True)

    def some_lists(step, carry):
        lists = [step * TOGETHER + i for i in group]
        f8, opac, off_x, start_y, mean_y, quad_a, quad_b, prec_y = ([None] * TOGETHER for _ in range(8))
        for i, l in enumerate(lists):
            number = tile * SCREENS + lax.rem(l, SCREENS)
            start_x = (16 * lax.rem(number, 8)).astype(f32) + 0.5
            start_y[i] = (16 * lax.div(number, 8)).astype(f32) + 0.5
            f8[i] = feat[l, 0:8, :]
            opac[i] = feat[l, 8:9, :] * live_ref[pl.ds(l, 1), :]
            off_x[i] = (sub16 + start_x) - f8[i][3:4, :]
            quad_a[i] = (half * f8[i][5:6, :]) * off_x[i] * off_x[i]
            quad_b[i] = (2.0 * half * f8[i][6:7, :]) * off_x[i]
            prec_y[i] = half * f8[i][7:8, :]
            mean_y[i] = f8[i][4:5, :]
        for y in range(16):
            rows = slice(16 * y, 16 * y + 16)
            for i in group:
                off_y = (start_y[i] + float(y)) - mean_y[i]
                quad = quad_a[i] + (off_y * quad_b[i] + prec_y[i] * off_y * off_y)
                a = opac[i] * jnp.exp2(quad)
                high, low = split(jnp.log(1.0 - a))
                alpha[i, rows, :] = a
                lk_h[i, rows, :] = high
                lk_l[i, rows, :] = low
        before = [before_ref[l] for l in lists]
        for c in range(4):
            rows = slice(64 * c, 64 * c + 64)
            for i in group:
                total = dot(lk_h[i, rows, :], before[i]) + dot(lk_l[i, rows, :], before[i])
                w = jnp.exp2(total * log2e) * alpha[i, rows, :]
                high, low = split(w)
                wgt[i, rows, :] = w
                wgt_h[i, rows, :] = high
                wgt_l[i, rows, :] = low
        left, right, d_h, d_l = ([None] * TOGETHER for _ in range(4))
        for i, l in enumerate(lists):
            c_h, c_l = split(f8[i])
            image = dot_t(c_h, wgt_h[i]) + (dot_t(c_h, wgt_l[i]) + dot_t(c_l, wgt_h[i]))
            goal8[i, 0:3, :] = goal_ref[0, l]
            diff = jnp.where(row8 < 3, image - goal8[i], 0.0)
            d_h[i], d_l[i] = split(diff)
            d_hf = d_h[i].astype(f32)
            d_lf = d_l[i].astype(f32)
            c_hf = c_h.astype(f32)
            c_lf = c_l.astype(f32)
            left[i] = jnp.transpose(jnp.concatenate([d_hf, d_hf, d_lf, d_lf], axis=0)).astype(bf16)
            right[i] = jnp.concatenate([c_hf, c_lf, c_hf, c_lf], axis=0).astype(bf16)
        for c in range(4):
            rows = slice(64 * c, 64 * c + 64)
            for i in group:
                u = wgt[i, rows, :] * dot(left[i][rows, :], right[i])
                high, low = split(u)
                u_f[i, rows, :] = u
                u_h[i, rows, :] = high
                u_l[i, rows, :] = low
        sums = [[jnp.zeros((16, SLOTS), f32) for _ in range(3)] for _ in group]
        for c in range(4):
            rows = slice(64 * c, 64 * c + 64)
            for i in group:
                later = dot_t(u_h[i, rows, :], before[i]) + dot_t(u_l[i, rows, :], before[i])
                a = alpha[i, rows, :]
                slope = u_f[i, rows, :] - later * (a / (1.0 - a))
                for y in range(4):
                    off_y = (start_y[i] + float(4 * c + y)) - mean_y[i]
                    part = slope[16 * y : 16 * y + 16, :]
                    moved = off_y * part
                    sums[i][0] = sums[i][0] + part
                    sums[i][1] = sums[i][1] + moved
                    sums[i][2] = sums[i][2] + off_y * moved
        for i, l in enumerate(lists):
            colour = dot(d_h[i], wgt_h[i]) + (dot(d_h[i], wgt_l[i]) + dot(d_l[i], wgt_h[i]))
            by_x = sums[i][0] * off_x[i]
            moments = (
                down(sums[i][0]),
                down(by_x),
                down(sums[i][1]),
                down(by_x * off_x[i]),
                down(sums[i][1] * off_x[i]),
            )
            for j in range(5):
                colour = jnp.where(row8 == 3 + j, moments[j], colour)
            grad[l] = colour
            grad8[pl.ds(l, 1), :] = down(sums[i][2])
        return carry

    lax.fori_loop(0, LISTS // TOGETHER, some_lists, 0)
    for h in range(2):
        lanes = slice(128 * h, 128 * (h + 1))
        whole = [grad[l, :, lanes] for l in range(LISTS)]
        ninth = grad8[:, lanes]
        for o in range(8):
            got = whole[o]
            for l in range(LISTS):
                if l != o:
                    got = jnp.where(block == l, pltpu.roll(whole[l], (l - o) * CAP % 128, 1), got)
            out_ref[8 * h + o, 0:8, :] = got
            last = jnp.where(row == block, lane_gather(ninth, inner + CAP * o), 0.0)
            out_ref[8 * h + o, 8:9, :] = jnp.sum(last, axis=0, keepdims=True)


def side_columns(x_ref, bidx_ref, a, e):
    index = jnp.broadcast_to(bidx_ref[0, e : e + 1, :], (8, NB))
    low = index & 127
    part = index >> 7
    got = [lane_gather(x_ref[a : a + 8, 128 * k : 128 * (k + 1)], low) for k in range(4)]
    return jnp.where(
        part < 2, jnp.where(part == 0, got[0], got[1]), jnp.where(part == 2, got[2], got[3])
    )


def update_kernel(
    step,
    last_round,
    centre_y,
    w_ref,
    cam_ref,
    gmsg_ref,
    *rest,
):
    if last_round:
        req_ref, *rest = rest
    (x_ref, m_ref, v_ref, bidx_ref, inv_ref, z_ref, u_ref), rest = rest[:7], rest[7:]
    (xo_ref, mo_ref, vo_ref, side_ref, sh0_ref, sh1_ref), rest = rest[:6], rest[6:]
    if last_round:
        wide, gin, gwide, terms, hits, prox, pad, grad = rest
    else:
        msg_ref, req_out, wide, feat, gin, gwide, terms, hits, prox, pad, grad = rest
    first = iota((ROWS, 128), 1) < 64
    sub_n = iota((SPL, 128), 0)
    for t in range(TILES):
        lanes = slice(128 * t, 128 * (t + 1))
        high, low = split(gmsg_ref[t])
        zero = jnp.zeros_like(high)
        terms[0:16, lanes] = jnp.where(first, high, zero)
        terms[16:32, lanes] = jnp.where(first, zero, high)
        terms[32:48, lanes] = jnp.where(first, low, zero)
        terms[48:64, lanes] = jnp.where(first, zero, low)
        if last_round:
            wanted = req_ref[t]
        else:
            wanted = gmsg_ref[t, 9:10, :].astype(i32)
            req_out[t] = wanted
        hits[:, lanes] = jnp.where(wanted == sub_n, 1.0, 0.0).astype(bf16)
    found = dot_t(terms[...], hits[...])
    total = found[0:32, :] + found[32:64, :]
    for v in range(2):
        for k in range(4):
            lanes = slice(128 * k, 128 * (k + 1))
            gin[pl.ds(4 * v + k, 8, stride=8), :] = total[16 * v : 16 * v + 8, lanes]
            gin[64 + 4 * v + k : 65 + 4 * v + k, :] = total[16 * v + 8 : 16 * v + 9, lanes]
    got = [gin[8 * f : 8 * f + 8, :] for f in range(FEATS)]

    pad[0:PARAMS, :] = x_ref[...]
    spread(x_ref, wide)
    cam = camera_of(cam_ref)
    centre = [wide_row(wide, i) for i in range(3)]
    log_scales = [wide_row(wide, 3 + i) for i in range(3)]
    quat = [wide_row(wide, 6 + i) for i in range(4)]
    coeffs = [wide_row(wide, 11 + i) for i in range(48)]
    geo, geo_back = jax.vjp(lambda a, b, c: geometry(a, b, c, cam), centre, log_scales, quat)
    p_xx, p_xy, p_yy = precision_of(geo[2], geo[3], geo[4])
    h_sum, m_x, m_y, m_xx, m_xy, m_yy = got[3:9]
    a_xx = p_xx * m_xx + p_xy * m_xy
    a_xy = p_xx * m_xy + p_xy * m_yy
    a_yx = p_xy * m_xx + p_yy * m_xy
    a_yy = p_xy * m_xy + p_yy * m_yy
    geo_grad = (
        p_xx * m_x + p_xy * m_y,
        p_xy * m_x + p_yy * m_y,
        0.5 * (a_xx * p_xx + a_xy * p_xy),
        a_xx * p_xy + a_xy * p_yy,
        0.5 * (a_yx * p_xy + a_yy * p_yy),
    )
    g_centre, g_scales, g_quat = geo_back(geo_grad)
    _, col_back = jax.vjp(lambda a, b: colours_of(a, b, cam), centre, coeffs)
    g_centre2, g_coeffs = col_back(list(got[0:3]))
    g_opac = h_sum * (1.0 - jax.nn.sigmoid(wide_row(wide, 10)))
    grads = (
        [g_centre[i] + g_centre2[i] for i in range(3)] + list(g_scales) + list(g_quat) + [g_opac] + list(g_coeffs)
    )
    for i in range(PARAMS):
        gwide[8 * i : 8 * i + 8, :] = grads[i]

    for a in range(0, PARAMS, 8):
        n = min(8, PARAMS - a)
        for e in range(2):
            mine = side_columns(pad, bidx_ref, a, e)[0:n]
            prox[a : a + n, NB * e : NB * (e + 1)] = (penalty * w_ref[e]) * (
                mine - z_ref[0, e, a : a + n, :] + u_ref[0, e, a : a + n, :]
            )
        for k in range(4):
            lanes = slice(128 * k, 128 * (k + 1))
            inverse = inv_ref[:, lanes]
            low = inverse & 127
            add = jnp.where(
                inverse < 128,
                lane_gather(prox[a : a + 8, 0:128], low),
                lane_gather(prox[a : a + 8, 128:256], low),
            )
            grad[a : a + 8, lanes] = (
                gwide[pl.ds(8 * a + k, 8, stride=8), :]
                + gwide[pl.ds(8 * a + 4 + k, 8, stride=8), :]
                + jnp.where(inverse >= 0, add, 0.0)
            )
    g = grad[0:PARAMS, :]
    m = beta_one * m_ref[...] + (1.0 - beta_one) * g
    v = beta_two * v_ref[...] + (1.0 - beta_two) * g * g
    corr_one = 1.0 - beta_one**step
    corr_two = 1.0 - beta_two**step
    x = x_ref[...] - (learn_rate / corr_one) * m / (jnp.sqrt(v * (1.0 / corr_two)) + adam_eps)
    mo_ref[...] = m
    vo_ref[...] = v
    xo_ref[...] = x
    pad[0:PARAMS, :] = x
    for a in range(0, PARAMS, 8):
        n = min(8, PARAMS - a)
        for e in range(2):
            mine = side_columns(pad, bidx_ref, a, e)[0:n]
            side_ref[e, a : a + n, :] = mine
            (sh0_ref, sh1_ref)[e][a : a + n, :] = mine + u_ref[0, e, a : a + n, :]
    if not last_round:
        spread(pad, wide)
        make_features(wide, cam, centre_y, feat)
        sources = sources_of(lambda rows: feat[rows, :])
        opac = feat[64:72, :]
        for t in range(TILES):
            main, last = pick_features(sources, opac, gmsg_ref[t, 9:10, :].astype(i32))
            msg_ref[t, 0:8, :] = main
            msg_ref[t, 8:9, :] = last


def consensus_kernel(w_ref, side_ref, u_ref, left_ref, right_ref, zo_ref, uo_ref):
    for e in range(2):
        w = w_ref[e]
        own = side_ref[e]
        dual = u_ref[0, e]
        agreed = w * (own + dual + (left_ref, right_ref)[e][...]) * 0.5 + (1.0 - w) * own
        zo_ref[:, e, :] = agreed
        uo_ref[:, e, :] = dual + w * (own - agreed)


def shape(dims, kind=f32):
    return jax.ShapeDtypeStruct(dims, kind)


def on_device(
    params, moment1, moment2, tile_lists, cameras, targets, boundary_index, links, consensus, duals
):
    block_total = lax.axis_size("block")
    tile_idx = lax.axis_index("tile")
    block_idx = lax.axis_index("block")
    centre_y = 8.0 * (TILES * SCREENS // 8)
    link_vals = links.astype(f32)
    right_w = jnp.where(block_idx < block_total - 1, link_vals[block_idx], 0.0)
    left_w = jnp.where(block_idx > 0, link_vals[jnp.maximum(block_idx - 1, 0)], 0.0)
    side_w = jnp.stack([left_w, right_w])
    tile_num = tile_idx.astype(i32).reshape(1)

    def call(kernel, name, outs, ins, scratch=()):
        return pl.pallas_call(
            kernel,
            out_shape=outs,
            in_specs=ins,
            out_specs=jax.tree.map(lambda _: ANY_VMEM, outs),
            scratch_shapes=list(scratch),
            compiler_params=pltpu.CompilerParams(vmem_limit_bytes=GRANT),
            name=name,
        )

    wide_scratch = VMEM((512, 128), f32)
    features = call(
        functools.partial(features_kernel, centre_y),
        "features",
        shape((WIDE, 128)),
        [ANY_VMEM, ANY_SMEM],
        [wide_scratch],
    )(params, cameras)
    message = lax.all_gather(features, "tile")
    before, live, wanted, inverse = call(
        lists_kernel,
        "lists",
        (
            shape((LISTS, SLOTS, SLOTS), bf16),
            shape((LISTS, SLOTS)),
            shape((TILES, 1, 128), i32),
            shape((8, SPL), i32),
        ),
        [ANY_VMEM] * 2,
    )(tile_lists, boundary_index)

    def exchange(value):
        return lax.all_to_all(value, "tile", 0, 0, tiled=True)

    def render(first_round):
        scratch = [
            VMEM((LISTS, 16, SLOTS), f32),
            VMEM((LISTS, 8, SLOTS), f32),
            VMEM((LISTS, SLOTS), f32),
            VMEM((TOGETHER, 8, SLOTS), f32),
        ]
        for kind in (f32, bf16, bf16, f32, bf16, bf16, f32, bf16, bf16):
            scratch.append(VMEM((TOGETHER, SLOTS, SLOTS), kind))
        if first_round:
            scratch.append(VMEM((TILES, ROWS, 128), f32))
        return call(
            functools.partial(render_kernel, first_round),
            "render",
            shape((TILES, ROWS, 128)),
            [ANY_SMEM] + [ANY_VMEM] * (5 if first_round else 4),
            scratch,
        )

    def shifted(x, by):
        pairs = [(i, i + by) for i in range(block_total) if 0 <= i + by < block_total]
        return lax.ppermute(x, "block", pairs)

    values, moment_one, moment_two = params, moment1, moment2
    agreed, dual_vars = consensus, duals
    requests = None
    for round_idx in range(ROUNDS):
        last_round = round_idx == ROUNDS - 1
        first_round = round_idx == 0
        if first_round:
            sent = render(True)(tile_num, message, before, live, targets, wanted)
        else:
            sent = render(False)(tile_num, exchange(message), before, live, targets)
        back = exchange(sent)
        outs = [shape((PARAMS, SPL))] * 3 + [shape((2, PARAMS, NB))] + [shape((PARAMS, NB))] * 2
        scratch = [wide_scratch]
        if not last_round:
            outs += [shape((TILES, ROWS, 128)), shape((TILES, 1, 128), i32)]
            scratch += [VMEM((WIDE, 128), f32)]
        scratch += [
            VMEM((WIDE, 128), f32),
            VMEM((512, 128), f32),
            VMEM((64, TILES * 128), bf16),
            VMEM((SPL, TILES * 128), bf16),
            VMEM((64, 2 * NB), f32),
            VMEM((64, SPL), f32),
            VMEM((64, SPL), f32),
        ]
        known = (requests,) if last_round else ()
        outs = call(
            functools.partial(update_kernel, first_step + round_idx + 1, last_round, centre_y),
            "update",
            tuple(outs),
            [ANY_SMEM, ANY_SMEM] + [ANY_VMEM] * (8 + len(known)),
            scratch,
        )(
            side_w,
            cameras,
            back,
            *known,
            values,
            moment_one,
            moment_two,
            boundary_index,
            inverse,
            agreed,
            dual_vars,
        )
        values, moment_one, moment_two, own_sides, shared0, shared1 = outs[:6]
        from_left = shifted(shared1, 1)
        from_right = shifted(shared0, -1)
        if not last_round:
            message, requests = outs[6:]
            partner = jnp.stack([from_left, from_right])[None]
            own_sides = own_sides[None]
            wide_w = side_w[None, :, None, None]
            agreed = wide_w * (own_sides + dual_vars + partner) * 0.5 + (1.0 - wide_w) * own_sides
            dual_vars = dual_vars + wide_w * (own_sides - agreed)
        else:
            sides = (shape((PARAMS, 2, NB)),) * 2
            sides = call(consensus_kernel, "consensus", sides, [ANY_SMEM] + [ANY_VMEM] * 4)(
                side_w, own_sides, dual_vars, from_left, from_right
            )
            agreed, dual_vars = (jnp.transpose(side, (1, 0, 2))[None] for side in sides)
    return (values, moment_one, moment_two, agreed, dual_vars)


def solution(mesh):
    both = ("block", "tile")
    placed = (
        P(None, both),
        P(None, both),
        P(None, both),
        P(both, None, None),
        P("block", None, None),
        P(both, None, None, None),
        P(both, None, None),
        P(),
        P(both, None, None, None),
        P(both, None, None, None),
    )
    return jax.shard_map(
        on_device,
        mesh=mesh,
        in_specs=placed,
        out_specs=(
            P(None, both),
            P(None, both),
            P(None, both),
            P(both, None, None, None),
            P(both, None, None, None),
        ),
        check_vma=False,
    )
```

```python
import functools
import jax
import jax.numpy as jnp
from jax import lax
from jax.experimental import pallas as pl
from jax.experimental.pallas import tpu as pltpu
from jax.sharding import PartitionSpec as P

PARAMS = 59
SCREENS = 4
ROUNDS = 2
LISTS = 8
CAP = 16
SLOTS = 256
TILES = 16
SPL = 512
NB = 128
ROWS = 16
FEATS = 9
WIDE = 72
BUFS = 2
CHUNK = 256
GRANT = 10 << 20

sh_zero = 0.28209479177387814
sh_one = 0.4886025119029199
sh_two = (
    1.0925484305920792,
    -1.0925484305920792,
    0.31539156525252005,
    -1.0925484305920792,
    0.5462742152960396,
)
sh_three = (
    -0.5900435899266435,
    2.890611442640554,
    -0.4570457994644658,
    0.3731763325901154,
    -0.4570457994644658,
    1.445305721320277,
    -0.5900435899266435,
)
beta_one = 0.9
beta_two = 0.999
learn_rate = 0.01
adam_eps = 1e-08
penalty = 2.0
first_step = 100
blur_var = 0.3
opacity_cap = 0.99
log2e = 1.4426950408889634

f32 = jnp.float32
bf16 = jnp.bfloat16
i32 = jnp.int32
VMEM = pltpu.VMEM
ANY_VMEM = pl.BlockSpec(memory_space=pltpu.VMEM)
ANY_SMEM = pl.BlockSpec(memory_space=pltpu.SMEM)


def iota(shape, axis):
    return lax.broadcasted_iota(i32, shape, axis)


def dot(a, b):
    return lax.dot_general(a, b, (((1,), (0,)), ((), ())), preferred_element_type=f32)


def dot_t(a, b):
    return lax.dot_general(a, b, (((1,), (1,)), ((), ())), preferred_element_type=f32)


def split(value):
    high = value.astype(bf16)
    return high, (value - high.astype(f32)).astype(bf16)


def lane_gather(value, index):
    return jnp.take_along_axis(value, index, axis=1, mode="promise_in_bounds")


def rotation(quat_w, quat_x, quat_y, quat_z):
    inverse = lax.rsqrt(quat_w * quat_w + quat_x * quat_x + quat_y * quat_y + quat_z * quat_z)
    unit_w = quat_w * inverse
    unit_x = quat_x * inverse
    unit_y = quat_y * inverse
    unit_z = quat_z * inverse
    return (
        (
            1.0 - 2.0 * (unit_y * unit_y + unit_z * unit_z),
            2.0 * (unit_x * unit_y - unit_w * unit_z),
            2.0 * (unit_x * unit_z + unit_w * unit_y),
        ),
        (
            2.0 * (unit_x * unit_y + unit_w * unit_z),
            1.0 - 2.0 * (unit_x * unit_x + unit_z * unit_z),
            2.0 * (unit_y * unit_z - unit_w * unit_x),
        ),
        (
            2.0 * (unit_x * unit_z - unit_w * unit_y),
            2.0 * (unit_y * unit_z + unit_w * unit_x),
            1.0 - 2.0 * (unit_x * unit_x + unit_y * unit_y),
        ),
    )


def sh_terms(dir_x, dir_y, dir_z):
    sq_x = dir_x * dir_x
    sq_y = dir_y * dir_y
    sq_z = dir_z * dir_z
    return (
        -sh_one * dir_y,
        sh_one * dir_z,
        -sh_one * dir_x,
        sh_two[0] * dir_x * dir_y,
        sh_two[1] * dir_y * dir_z,
        sh_two[2] * (2.0 * sq_z - sq_x - sq_y),
        sh_two[3] * dir_x * dir_z,
        sh_two[4] * (sq_x - sq_y),
        sh_three[0] * dir_y * (3.0 * sq_x - sq_y),
        sh_three[1] * dir_x * dir_y * dir_z,
        sh_three[2] * dir_y * (4.0 * sq_z - sq_x - sq_y),
        sh_three[3] * dir_z * (2.0 * sq_z - 3.0 * sq_x - 3.0 * sq_y),
        sh_three[4] * dir_x * (4.0 * sq_z - sq_x - sq_y),
        sh_three[5] * dir_z * (sq_x - sq_y),
        sh_three[6] * dir_x * (sq_x - 3.0 * sq_y),
    )


def camera_of(cam_ref):
    first = iota((8, 128), 0) < 4
    vals = [jnp.where(first, cam_ref[0, 0, i], cam_ref[0, 1, i]) for i in range(8)]
    rot = rotation(vals[0], vals[1], vals[2], vals[3])
    shift = vals[4:7]
    eye = [-(rot[0][c] * shift[0] + rot[1][c] * shift[1] + rot[2][c] * shift[2]) for c in range(3)]
    return rot, shift, vals[7], eye


def geometry(centre, log_scales, quat, cam):
    cam_rot, shift, focal, _ = cam
    in_cam = [
        cam_rot[r][0] * centre[0] + cam_rot[r][1] * centre[1] + cam_rot[r][2] * centre[2] + shift[r]
        for r in range(3)
    ]
    inv_depth = 1.0 / in_cam[2]
    scaled = focal * inv_depth
    ratio_x = in_cam[0] * inv_depth
    ratio_y = in_cam[1] * inv_depth
    mean_x = focal * ratio_x
    mean_y = focal * ratio_y
    screen_map = [
        [scaled * (cam_rot[0][c] - ratio_x * cam_rot[2][c]) for c in range(3)],
        [scaled * (cam_rot[1][c] - ratio_y * cam_rot[2][c]) for c in range(3)],
    ]
    local_rot = rotation(*quat)
    scales = [jnp.exp(s) for s in log_scales]
    axes = [
        [
            (
                screen_map[r][0] * local_rot[0][c]
                + screen_map[r][1] * local_rot[1][c]
                + screen_map[r][2] * local_rot[2][c]
            )
            * scales[c]
            for c in range(3)
        ]
        for r in range(2)
    ]
    cov_xx = axes[0][0] * axes[0][0] + axes[0][1] * axes[0][1] + axes[0][2] * axes[0][2] + blur_var
    cov_xy = axes[0][0] * axes[1][0] + axes[0][1] * axes[1][1] + axes[0][2] * axes[1][2]
    cov_yy = axes[1][0] * axes[1][0] + axes[1][1] * axes[1][1] + axes[1][2] * axes[1][2] + blur_var
    return mean_x, mean_y, cov_xx, cov_xy, cov_yy


def colours_of(centre, coeffs, cam):
    eye = cam[3]
    view = [centre[c] - eye[c] for c in range(3)]
    inverse = lax.rsqrt(view[0] * view[0] + view[1] * view[1] + view[2] * view[2])
    terms = sh_terms(view[0] * inverse, view[1] * inverse, view[2] * inverse)
    out = []
    for ch in range(3):
        total = sh_zero * coeffs[ch] + 0.5
        for q in range(15):
            total = total + terms[q] * coeffs[3 * (q + 1) + ch]
        out.append(total)
    return out


def precision_of(cov_xx, cov_xy, cov_yy):
    inverse = 1.0 / (cov_xx * cov_yy - cov_xy * cov_xy)
    return cov_yy * inverse, -cov_xy * inverse, cov_xx * inverse


def spread(x_ref, wide):
    for a in range(0, PARAMS, 8):
        n = min(8, PARAMS - a)
        for k in range(4):
            piece = x_ref[a : a + n, 128 * k : 128 * (k + 1)]
            for v in range(2):
                wide[pl.ds(8 * a + 4 * v + k, n, stride=8), :] = piece


def wide_row(wide, i):
    return wide[8 * i : 8 * i + 8, :]


def make_features(wide, cam, centre_y, feat):
    centre = [wide_row(wide, i) for i in range(3)]
    geo = geometry(
        centre, [wide_row(wide, 3 + i) for i in range(3)], [wide_row(wide, 6 + i) for i in range(4)], cam
    )
    prec = precision_of(geo[2], geo[3], geo[4])
    cols = colours_of(centre, [wide_row(wide, 11 + i) for i in range(48)], cam)
    opac = opacity_cap * jax.nn.sigmoid(wide_row(wide, 10))
    values = (*cols, geo[0] + 64.0, geo[1] + centre_y, *prec, opac)
    for f in range(FEATS):
        feat[8 * f : 8 * f + 8, :] = values[f]


def pick_features(sources, opac, index_row):
    row = iota((8, 128), 0)
    first = iota((8, 128), 1) < 64
    index = jnp.broadcast_to(jnp.maximum(index_row, 0), (8, 128))
    low = index & 127
    part = index >> 7
    both = []
    for v in range(2):
        got = [lane_gather(sources[v][k], low) for k in range(4)]
        both.append(
            jnp.where(part < 2, jnp.where(part == 0, got[0], got[1]), jnp.where(part == 2, got[2], got[3]))
        )
    last = jnp.where(row == jnp.where(first, 0, 4) + part, lane_gather(opac, low), 0.0)
    return jnp.where(first, both[0], both[1]), jnp.sum(last, axis=0, keepdims=True)


def sources_of(load):
    return [[load(pl.ds(4 * v + k, 8, stride=8)) for k in range(4)] for v in range(2)]


def lists_kernel(lists_ref, bidx_ref, before_ref, live_ref, req_ref, inv_ref):
    sub = iota((SLOTS, SLOTS), 0)
    lane = iota((SLOTS, SLOTS), 1)
    upto = jnp.where(sub <= lane, 1.0, 0.0).astype(bf16)
    number = (iota((SLOTS, 128), 0) + 1).astype(f32).astype(bf16)
    slot = iota((1, SLOTS), 1)
    row8 = iota((8, SLOTS), 0)
    owners = iota((TILES, SLOTS), 0)
    row = iota((8, 128), 0)
    col = iota((8, 128), 1)
    pick = row * CAP + (col & (CAP - 1))
    acc = [jnp.full((8, 128), -1, i32) for _ in range(2)]
    for l in range(LISTS):
        ids = lists_ref[0, l : l + 1, :]
        live = ids >= 0
        owner = jnp.where(live, ids >> 9, -1)
        local = ids & (SPL - 1)
        mine = owner == owners
        counts = dot(jnp.where(mine, 1.0, 0.0).astype(bf16), upto)
        rank = jnp.sum(jnp.where(mine, counts, 0.0), axis=0, keepdims=True).astype(i32) - 1
        place = jnp.where(live, owner * CAP + rank, -1)
        chosen = jnp.where(place == sub, 1.0, 0.0).astype(bf16)
        rows = jnp.where(
            row8 == 0, slot + 1, jnp.where(row8 == 1, local & 255, jnp.where(row8 == 2, local >> 8, 0))
        )
        found = dot_t(rows.astype(f32).astype(bf16), chosen)
        order = found[0:1, :]
        column = dot(chosen, number)
        before_ref[l] = jnp.where(jnp.concatenate([column, column], axis=1) < order, 1.0, 0.0).astype(bf16)
        held = order > 0.5
        live_ref[l : l + 1, :] = jnp.where(held, 1.0, 0.0)
        wanted = jnp.where(held, found[1:2, :] + 256.0 * found[2:3, :], -1.0).astype(i32)
        for h in range(2):
            half = jnp.broadcast_to(wanted[:, 128 * h : 128 * (h + 1)], (8, 128))
            acc[h] = jnp.where((col >> 4) == l, lane_gather(half, pick), acc[h])
    for o in range(TILES):
        req_ref[o] = acc[o // 8][o % 8 : o % 8 + 1, :]
    total = jnp.zeros((8, SPL), f32)
    sub_n = iota((SPL, NB), 0)
    for e in range(2):
        hit = jnp.where(bidx_ref[0, e : e + 1, :] == sub_n, 1.0, 0.0).astype(bf16)
        total = total + dot_t((col + (NB * e + 1)).astype(f32).astype(bf16), hit)
    inv_ref[...] = total.astype(i32) - 1


def start_kernel(
    centre_y,
    lists_hbm,
    bidx_hbm,
    x_hbm,
    cam_hbm,
    feat_ref,
    before_ref,
    live_ref,
    req_ref,
    inv_ref,
    lists,
    bidx,
    x,
    cam,
    wide,
    sems,
):
    pairs = ((lists_hbm, lists), (bidx_hbm, bidx), (x_hbm, x), (cam_hbm, cam))
    copies = [pltpu.make_async_copy(a, b, sems.at[i]) for i, (a, b) in enumerate(pairs)]
    for copy in copies:
        copy.start()
    copies[0].wait()
    copies[1].wait()
    lists_kernel(lists, bidx, before_ref, live_ref, req_ref, inv_ref)
    copies[2].wait()
    copies[3].wait()
    spread(x, wide)
    make_features(wide, camera_of(cam), centre_y, feat_ref)


def render_kernel(
    first_round,
    tile_ref,
    msg_in,
    before_ref,
    live_ref,
    goal_ref,
    *rest,
):
    if first_round:
        req_ref, out_ref, msg_ref = rest[0], rest[1], rest[-1]
        rest = rest[2:-1]
        for o in range(TILES):
            main, last = pick_features(
                sources_of(lambda rows: msg_in[o, rows, :]), msg_in[o, 64:72, :], req_ref[o]
            )
            msg_ref[ROWS * o : ROWS * o + 8, :] = main
            msg_ref[ROWS * o + 8 : ROWS * o + 9, :] = last
            out_ref[10 * o + 9 : 10 * o + 10, :] = req_ref[o].astype(f32)
    else:
        msg_ref, out_ref = msg_in, rest[0]
        rest = rest[1:]
    rows_in = ROWS if first_round else FEATS
    rows_out = FEATS + first_round
    feat, grad, grad8, goal8, alpha, lk_h, lk_l, wgt, wgt_h, wgt_l, u_f, u_h, u_l = rest
    row = iota((8, 128), 0)
    col = iota((8, 128), 1)
    block = col >> 4
    inner = col & (CAP - 1)
    for h in range(2):
        starts = [rows_in * (8 * h + o) for o in range(8)]
        whole = [msg_ref[at : at + 8, :] for at in starts]
        ninth = jnp.concatenate([msg_ref[at + 8 : at + 9, :] for at in starts], axis=0)
        for l in range(LISTS):
            got = whole[l]
            for o in range(8):
                if o != l:
                    got = jnp.where(block == o, pltpu.roll(whole[o], (o - l) * CAP % 128, 1), got)
            feat[l, 0:8, 128 * h : 128 * (h + 1)] = got
            last = jnp.where(row == block, lane_gather(ninth, inner + CAP * l), 0.0)
            feat[l, 8:9, 128 * h : 128 * (h + 1)] = jnp.sum(last, axis=0, keepdims=True)
    goal8[...] = jnp.zeros_like(goal8)
    tile = tile_ref[0]
    sub16 = iota((16, SLOTS), 0).astype(f32)
    row8 = iota((8, SLOTS), 0)
    half = -0.5 * log2e
    down = functools.partial(jnp.sum, axis=0, keepdims=True)
    state = [None] * LISTS

    def front(l):
        b = l % BUFS
        number = tile * SCREENS + l % SCREENS
        start_x = (16 * lax.rem(number, 8)).astype(f32) + 0.5
        start_y = (16 * lax.div(number, 8)).astype(f32) + 0.5
        f8 = feat[l, 0:8, :]
        opac = feat[l, 8:9, :] * live_ref[l : l + 1, :]
        off_x = (sub16 + start_x) - f8[3:4, :]
        quad_a = (half * f8[5:6, :]) * off_x * off_x
        quad_b = (2.0 * half * f8[6:7, :]) * off_x
        prec_y = half * f8[7:8, :]
        mean_y = f8[4:5, :]
        state[l] = (f8, off_x, start_y, mean_y)
        for at in range(0, SLOTS, CHUNK):
            for y in range(at // 16, (at + CHUNK) // 16):
                rows = slice(16 * y, 16 * y + 16)
                off_y = (start_y + float(y)) - mean_y
                quad = quad_a + (off_y * quad_b + prec_y * off_y * off_y)
                a = opac * jnp.exp2(quad)
                high, low = split(jnp.log(1.0 - a))
                alpha[b, rows, :] = a
                lk_h[b, rows, :] = high
                lk_l[b, rows, :] = low
                if y % 4 == 3:
                    yield
            rows = slice(at, at + CHUNK)
            before = before_ref[l]
            total = dot(lk_h[b, rows, :], before) + dot(lk_l[b, rows, :], before)
            for sub in range(0, CHUNK, 32):
                rows = slice(at + sub, at + sub + 32)
                w = jnp.exp2(total[sub : sub + 32] * log2e) * alpha[b, rows, :]
                high, low = split(w)
                wgt[b, rows, :] = w
                wgt_h[b, rows, :] = high
                wgt_l[b, rows, :] = low
            yield

    def back(l):
        b = l % BUFS
        f8, off_x, start_y, mean_y = state[l]
        c_h, c_l = split(f8)
        c_hf = c_h.astype(f32)
        c_lf = c_l.astype(f32)
        c_both = jnp.concatenate([c_hf, c_lf], axis=0).astype(bf16)
        image = dot_t(c_both, wgt_h[b])
        image = image[0:8] + (image[8:16] + dot_t(c_h, wgt_l[b]))
        yield
        for ch in range(3):
            goal8[b, ch : ch + 1, :] = goal_ref[0, ch, l : l + 1, :]
        diff = jnp.where(row8 < 3, image - goal8[b], 0.0)
        d_h, d_l = split(diff)
        d_hf = d_h.astype(f32)
        d_lf = d_l.astype(f32)
        d_both = jnp.concatenate([d_hf, d_lf], axis=0).astype(bf16)
        left = jnp.transpose(jnp.concatenate([d_hf, d_hf, d_lf, d_lf], axis=0)).astype(bf16)
        right = jnp.concatenate([c_hf, c_lf, c_hf, c_lf], axis=0).astype(bf16)
        yield
        sums = [jnp.zeros((16, SLOTS), f32) for _ in range(3)]
        before = before_ref[l]
        for at in range(0, SLOTS, CHUNK):
            slopes = dot(left[at : at + CHUNK], right)
            for sub in range(0, CHUNK, 32):
                rows = slice(at + sub, at + sub + 32)
                u = wgt[b, rows, :] * slopes[sub : sub + 32]
                high, low = split(u)
                u_f[b, rows, :] = u
                u_h[b, rows, :] = high
                u_l[b, rows, :] = low
            yield
            rows = slice(at, at + CHUNK)
            later = dot_t(u_h[b, rows, :], before) + dot_t(u_l[b, rows, :], before)
            for sub in range(0, CHUNK, 16):
                rows = slice(at + sub, at + sub + 16)
                a = alpha[b, rows, :]
                part = u_f[b, rows, :] - later[sub : sub + 16] * (a / (1.0 - a))
                off_y = (start_y + float((at + sub) // 16)) - mean_y
                moved = off_y * part
                sums[0] = sums[0] + part
                sums[1] = sums[1] + moved
                sums[2] = sums[2] + off_y * moved
                if sub % 64 == 48:
                    yield
        colour = dot(d_both, wgt_h[b])
        colour = colour[0:8] + (colour[8:16] + dot(d_h, wgt_l[b]))
        by_x = sums[0] * off_x
        moments = (
            down(sums[0]),
            down(by_x),
            down(sums[1]),
            down(by_x * off_x),
            down(sums[1] * off_x),
        )
        for i in range(5):
            colour = jnp.where(row8 == 3 + i, moments[i], colour)
        grad[l] = colour
        grad8[l : l + 1, :] = down(sums[2])
        yield

    for l in range(LISTS + 1):
        streams = ([back(l - 1)] if l > 0 else []) + ([front(l)] if l < LISTS else [])
        while streams:
            streams = [stream for stream in streams if next(stream, streams) is None]

    for h in range(2):
        lanes = slice(128 * h, 128 * (h + 1))
        whole = [grad[l, :, lanes] for l in range(LISTS)]
        ninth = grad8[:, lanes]
        for o in range(8):
            got = whole[o]
            for l in range(LISTS):
                if l != o:
                    got = jnp.where(block == l, pltpu.roll(whole[l], (l - o) * CAP % 128, 1), got)
            at = rows_out * (8 * h + o)
            out_ref[at : at + 8, :] = got
            last = jnp.where(row == block, lane_gather(ninth, inner + CAP * o), 0.0)
            out_ref[at + 8 : at + 9, :] = jnp.sum(last, axis=0, keepdims=True)


def side_columns(x_ref, bidx_ref, a, e):
    index = jnp.broadcast_to(bidx_ref[0, e : e + 1, :], (8, NB))
    low = index & 127
    part = index >> 7
    got = [lane_gather(x_ref[a : a + 8, 128 * k : 128 * (k + 1)], low) for k in range(4)]
    return jnp.where(
        part < 2, jnp.where(part == 0, got[0], got[1]), jnp.where(part == 2, got[2], got[3])
    )


def adam(step, g, x, m, v):
    m = beta_one * m + (1.0 - beta_one) * g
    v = beta_two * v + (1.0 - beta_two) * g * g
    corr_one = 1.0 - beta_one**step
    corr_two = 1.0 - beta_two**step
    x = x - (learn_rate / corr_one) * m / (jnp.sqrt(v * (1.0 / corr_two)) + adam_eps)
    return x, m, v


def adam_kernel(step, g_ref, x_ref, m_ref, v_ref, xo_ref, mo_ref, vo_ref):
    xo_ref[...], mo_ref[...], vo_ref[...] = adam(step, g_ref[...], x_ref[...], m_ref[...], v_ref[...])


def update_kernel(
    step,
    last_round,
    centre_y,
    w_ref,
    cam_ref,
    gmsg_ref,
    *rest,
):
    if last_round:
        req_ref, *rest = rest
    (x_ref, m_ref, v_ref, bidx_ref, inv_ref, z_ref, u_ref), rest = rest[:7], rest[7:]
    if last_round:
        g_ref, *rest = rest
    else:
        (xo_ref, mo_ref, vo_ref), rest = rest[:3], rest[3:]
    (side_ref, near_ref, far_ref), rest = rest[:3], rest[3:]
    if last_round:
        wide, gin, gwide, terms, hits, prox, pad, grad = rest
    else:
        msg_ref, req_out, wide, feat, gin, gwide, terms, hits, prox, pad, grad = rest
    rows_in = FEATS if last_round else FEATS + 1
    first = iota((ROWS, 128), 1) < 64
    sub_n = iota((SPL, 128), 0)
    for t in range(TILES):
        lanes = slice(128 * t, 128 * (t + 1))
        at = rows_in * t
        ninth = jnp.broadcast_to(gmsg_ref[at + 8 : at + 9, :], (8, 128))
        high, low = split(jnp.concatenate([gmsg_ref[at : at + 8, :], ninth], axis=0))
        zero = jnp.zeros_like(high)
        terms[0:16, lanes] = jnp.where(first, high, zero)
        terms[16:32, lanes] = jnp.where(first, zero, high)
        terms[32:48, lanes] = jnp.where(first, low, zero)
        terms[48:64, lanes] = jnp.where(first, zero, low)
        if last_round:
            wanted = req_ref[t]
        else:
            wanted = gmsg_ref[at + 9 : at + 10, :].astype(i32)
            req_out[t] = wanted
        hits[:, lanes] = jnp.where(wanted == sub_n, 1.0, 0.0).astype(bf16)
    found = dot_t(terms[...], hits[...])
    total = found[0:32, :] + found[32:64, :]
    for v in range(2):
        for k in range(4):
            lanes = slice(128 * k, 128 * (k + 1))
            gin[pl.ds(4 * v + k, 8, stride=8), :] = total[16 * v : 16 * v + 8, lanes]
            gin[64 + 4 * v + k : 65 + 4 * v + k, :] = total[16 * v + 8 : 16 * v + 9, lanes]
    got = [gin[8 * f : 8 * f + 8, :] for f in range(FEATS)]

    pad[0:PARAMS, :] = x_ref[...]
    spread(x_ref, wide)
    cam = camera_of(cam_ref)
    centre = [wide_row(wide, i) for i in range(3)]
    log_scales = [wide_row(wide, 3 + i) for i in range(3)]
    quat = [wide_row(wide, 6 + i) for i in range(4)]
    coeffs = [wide_row(wide, 11 + i) for i in range(48)]
    geo, geo_back = jax.vjp(lambda a, b, c: geometry(a, b, c, cam), centre, log_scales, quat)
    p_xx, p_xy, p_yy = precision_of(geo[2], geo[3], geo[4])
    h_sum, m_x, m_y, m_xx, m_xy, m_yy = got[3:9]
    a_xx = p_xx * m_xx + p_xy * m_xy
    a_xy = p_xx * m_xy + p_xy * m_yy
    a_yx = p_xy * m_xx + p_yy * m_xy
    a_yy = p_xy * m_xy + p_yy * m_yy
    geo_grad = (
        p_xx * m_x + p_xy * m_y,
        p_xy * m_x + p_yy * m_y,
        0.5 * (a_xx * p_xx + a_xy * p_xy),
        a_xx * p_xy + a_xy * p_yy,
        0.5 * (a_yx * p_xy + a_yy * p_yy),
    )
    g_centre, g_scales, g_quat = geo_back(geo_grad)
    _, col_back = jax.vjp(lambda a, b: colours_of(a, b, cam), centre, coeffs)
    g_centre2, g_coeffs = col_back(list(got[0:3]))
    g_opac = h_sum * (1.0 - jax.nn.sigmoid(wide_row(wide, 10)))
    grads = (
        [g_centre[i] + g_centre2[i] for i in range(3)] + list(g_scales) + list(g_quat) + [g_opac] + list(g_coeffs)
    )
    for i in range(PARAMS):
        gwide[8 * i : 8 * i + 8, :] = grads[i]

    for a in range(0, PARAMS, 8):
        n = min(8, PARAMS - a)
        for e in range(2):
            mine = side_columns(pad, bidx_ref, a, e)[0:n]
            prox[a : a + n, NB * e : NB * (e + 1)] = (penalty * w_ref[e]) * (
                mine - z_ref[0, e, a : a + n, :] + u_ref[0, e, a : a + n, :]
            )
        for k in range(4):
            lanes = slice(128 * k, 128 * (k + 1))
            inverse = inv_ref[:, lanes]
            low = inverse & 127
            add = jnp.where(
                inverse < 128,
                lane_gather(prox[a : a + 8, 0:128], low),
                lane_gather(prox[a : a + 8, 128:256], low),
            )
            grad[a : a + 8, lanes] = (
                gwide[pl.ds(8 * a + k, 8, stride=8), :]
                + gwide[pl.ds(8 * a + 4 + k, 8, stride=8), :]
                + jnp.where(inverse >= 0, add, 0.0)
            )
    x, m, v = adam(step, grad[0:PARAMS, :], x_ref[...], m_ref[...], v_ref[...])
    if last_round:
        g_ref[...] = grad[0:PARAMS, :]
    else:
        xo_ref[...] = x
        mo_ref[...] = m
        vo_ref[...] = v
    pad[0:PARAMS, :] = x
    even = w_ref[2] > 0.5
    for a in range(0, PARAMS, 8):
        n = min(8, PARAMS - a)
        shared = []
        for e in range(2):
            mine = side_columns(pad, bidx_ref, a, e)[0:n]
            side_ref[e, a : a + n, :] = mine
            shared.append(mine + u_ref[0, e, a : a + n, :])
        near_ref[a : a + n, :] = jnp.where(even, shared[1], shared[0])
        far_ref[a : a + n, :] = jnp.where(even, shared[0], shared[1])
    if not last_round:
        spread(pad, wide)
        make_features(wide, cam, centre_y, feat)
        sources = sources_of(lambda rows: feat[rows, :])
        opac = feat[64:72, :]
        for t in range(TILES):
            main, last = pick_features(
                sources, opac, gmsg_ref[rows_in * t + 9 : rows_in * t + 10, :].astype(i32)
            )
            msg_ref[FEATS * t : FEATS * t + 8, :] = main
            msg_ref[FEATS * t + 8 : FEATS * t + 9, :] = last


def consensus_kernel(w_ref, side_ref, u_ref, near_ref, far_ref, zo_ref, uo_ref):
    even = w_ref[2] > 0.5
    near = near_ref[...]
    far = far_ref[...]
    partner = (jnp.where(even, far, near), jnp.where(even, near, far))
    for e in range(2):
        w = w_ref[e]
        own = side_ref[e]
        dual = u_ref[0, e]
        agreed = w * (own + dual + partner[e]) * 0.5 + (1.0 - w) * own
        zo_ref[:, e, :] = agreed
        uo_ref[:, e, :] = dual + w * (own - agreed)


def shape(dims, kind=f32):
    return jax.ShapeDtypeStruct(dims, kind)


def on_device(
    params, moment1, moment2, tile_lists, cameras, targets, boundary_index, links, consensus, duals
):
    block_total = lax.axis_size("block")
    tile_idx = lax.axis_index("tile")
    block_idx = lax.axis_index("block")
    centre_y = 8.0 * (TILES * SCREENS // 8)
    link_vals = links.astype(f32)
    right_w = jnp.where(block_idx < block_total - 1, link_vals[block_idx], 0.0)
    left_w = jnp.where(block_idx > 0, link_vals[jnp.maximum(block_idx - 1, 0)], 0.0)
    even = block_idx % 2 == 0
    side_w = jnp.stack([left_w, right_w, jnp.where(even, 1.0, 0.0)])
    goals = jnp.transpose(targets, (0, 2, 1, 3))
    tile_num = tile_idx.astype(i32).reshape(1)

    def call(kernel, outs, ins, scratch=()):
        return pl.pallas_call(
            kernel,
            out_shape=outs,
            in_specs=ins,
            out_specs=jax.tree.map(lambda _: ANY_VMEM, outs),
            scratch_shapes=list(scratch),
            compiler_params=pltpu.CompilerParams(vmem_limit_bytes=GRANT),
        )

    wide_scratch = VMEM((512, 128), f32)
    features, before, live, wanted, inverse = call(
        functools.partial(start_kernel, centre_y),
        (
            shape((WIDE, 128)),
            shape((LISTS, SLOTS, SLOTS), bf16),
            shape((LISTS, SLOTS)),
            shape((TILES, 1, 128), i32),
            shape((8, SPL), i32),
        ),
        [pl.BlockSpec(memory_space=pltpu.HBM)] * 4,
        [
            VMEM((1, LISTS, SLOTS), i32),
            VMEM((1, 2, NB), i32),
            VMEM((PARAMS, SPL), f32),
            pltpu.SMEM((1, 2, 8), f32),
            wide_scratch,
            pltpu.SemaphoreType.DMA((4,)),
        ],
    )(tile_lists, boundary_index, params, cameras)
    message = lax.all_gather(features, "tile")

    def exchange(value, rows):
        moved = lax.all_to_all(value.reshape(TILES, 1, rows * 128), "tile", 0, 0, tiled=True)
        return moved.reshape(TILES * rows, 128)

    def render(first_round):
        scratch = [
            VMEM((LISTS, 16, SLOTS), f32),
            VMEM((LISTS, 8, SLOTS), f32),
            VMEM((LISTS, SLOTS), f32),
            VMEM((BUFS, 8, SLOTS), f32),
        ]
        for kind in (f32, bf16, bf16, f32, bf16, bf16, f32, bf16, bf16):
            scratch.append(VMEM((BUFS, SLOTS, SLOTS), kind))
        if first_round:
            scratch.append(VMEM((TILES * ROWS, 128), f32))
        return call(
            functools.partial(render_kernel, first_round),
            shape((TILES * (FEATS + first_round), 128)),
            [ANY_SMEM] + [ANY_VMEM] * (5 if first_round else 4),
            scratch,
        )

    def swapped(x, first):
        pairs = [(i, i + 1) for i in range(first, block_total - 1, 2)]
        return lax.ppermute(x, "block", pairs + [(j, i) for i, j in pairs])

    values, moment_one, moment_two = params, moment1, moment2
    agreed, dual_vars = consensus, duals
    requests = None
    for round_idx in range(ROUNDS):
        last_round = round_idx == ROUNDS - 1
        first_round = round_idx == 0
        if first_round:
            sent = render(True)(tile_num, message, before, live, goals, wanted)
        else:
            received = exchange(message, FEATS)
            sent = render(False)(tile_num, received, before, live, goals)
        back = exchange(sent, FEATS + first_round)
        outs = [shape((PARAMS, SPL))] * (1 if last_round else 3)
        outs += [shape((2, PARAMS, NB))] + [shape((PARAMS, NB))] * 2
        scratch = [wide_scratch]
        if not last_round:
            outs += [shape((TILES * FEATS, 128)), shape((TILES, 1, 128), i32)]
            scratch += [VMEM((WIDE, 128), f32)]
        scratch += [
            VMEM((WIDE, 128), f32),
            VMEM((512, 128), f32),
            VMEM((64, TILES * 128), bf16),
            VMEM((SPL, TILES * 128), bf16),
            VMEM((64, 2 * NB), f32),
            VMEM((64, SPL), f32),
            VMEM((64, SPL), f32),
        ]
        known = (requests,) if last_round else ()
        outs = call(
            functools.partial(update_kernel, first_step + round_idx + 1, last_round, centre_y),
            tuple(outs),
            [ANY_SMEM, ANY_SMEM] + [ANY_VMEM] * (8 + len(known)),
            scratch,
        )(
            side_w,
            cameras,
            back,
            *known,
            values,
            moment_one,
            moment_two,
            boundary_index,
            inverse,
            agreed,
            dual_vars,
        )
        if last_round:
            grads, own_sides, near, far = outs
        else:
            *changed, own_sides, near, far, message, requests = outs
        far = swapped(far, 1)
        near = swapped(near, 0)
        if not last_round:
            values, moment_one, moment_two = changed
            partner = jnp.stack([jnp.where(even, far, near), jnp.where(even, near, far)])[None]
            own_sides = own_sides[None]
            wide_w = side_w[None, :2, None, None]
            agreed = wide_w * (own_sides + dual_vars + partner) * 0.5 + (1.0 - wide_w) * own_sides
            dual_vars = dual_vars + wide_w * (own_sides - agreed)
        else:
            values, moment_one, moment_two = call(
                functools.partial(adam_kernel, first_step + ROUNDS),
                (shape((PARAMS, SPL)),) * 3,
                [ANY_VMEM] * 4,
            )(grads, values, moment_one, moment_two)
            sides = (shape((PARAMS, 2, NB)),) * 2
            sides = call(consensus_kernel, sides, [ANY_SMEM] + [ANY_VMEM] * 4)(
                side_w, own_sides, dual_vars, near, far
            )
            agreed, dual_vars = (jnp.transpose(side, (1, 0, 2))[None] for side in sides)
    return (values, moment_one, moment_two, agreed, dual_vars)


def solution(mesh):
    both = ("block", "tile")
    placed = (
        P(None, both),
        P(None, both),
        P(None, both),
        P(both, None, None),
        P("block", None, None),
        P(both, None, None, None),
        P(both, None, None),
        P(),
        P(both, None, None, None),
        P(both, None, None, None),
    )
    return jax.shard_map(
        on_device,
        mesh=mesh,
        in_specs=placed,
        out_specs=(
            P(None, both),
            P(None, both),
            P(None, both),
            P(both, None, None, None),
            P(both, None, None, None),
        ),
        check_vma=False,
    )
```

```python
import functools
import jax
import jax.numpy as jnp
from jax import lax
from jax.experimental import pallas as pl
from jax.experimental.pallas import tpu as pltpu
from jax.sharding import PartitionSpec as P

PARAMS = 59
SCREENS = 4
ROUNDS = 2
LISTS = 8
CAP = 16
SLOTS = 256
TILES = 16
SPL = 512
NB = 128
ROWS = 16
FEATS = 9
WIDE = 72
BUFS = 2
CHUNK = 256
GRANT = 10 << 20
MICROS = {"lists": 2, "features": 1, "render": 6, "update": 2, "prox": 1, "adam": 1, "consensus": 1}

sh_zero = 0.28209479177387814
sh_one = 0.4886025119029199
sh_two = (
    1.0925484305920792,
    -1.0925484305920792,
    0.31539156525252005,
    -1.0925484305920792,
    0.5462742152960396,
)
sh_three = (
    -0.5900435899266435,
    2.890611442640554,
    -0.4570457994644658,
    0.3731763325901154,
    -0.4570457994644658,
    1.445305721320277,
    -0.5900435899266435,
)
beta_one = 0.9
beta_two = 0.999
learn_rate = 0.01
adam_eps = 1e-08
penalty = 2.0
first_step = 100
blur_var = 0.3
opacity_cap = 0.99
log2e = 1.4426950408889634

f32 = jnp.float32
bf16 = jnp.bfloat16
i32 = jnp.int32
VMEM = pltpu.VMEM
ANY_VMEM = pl.BlockSpec(memory_space=pltpu.VMEM)
ANY_SMEM = pl.BlockSpec(memory_space=pltpu.SMEM)


def iota(shape, axis):
    return lax.broadcasted_iota(i32, shape, axis)


def dot(a, b):
    return lax.dot_general(a, b, (((1,), (0,)), ((), ())), preferred_element_type=f32)


def dot_t(a, b):
    return lax.dot_general(a, b, (((1,), (1,)), ((), ())), preferred_element_type=f32)


def split(value):
    high = value.astype(bf16)
    return high, (value - high.astype(f32)).astype(bf16)


def lane_gather(value, index):
    return jnp.take_along_axis(value, index, axis=1, mode="promise_in_bounds")


def rotation(quat_w, quat_x, quat_y, quat_z):
    inverse = lax.rsqrt(quat_w * quat_w + quat_x * quat_x + quat_y * quat_y + quat_z * quat_z)
    unit_w = quat_w * inverse
    unit_x = quat_x * inverse
    unit_y = quat_y * inverse
    unit_z = quat_z * inverse
    return (
        (
            1.0 - 2.0 * (unit_y * unit_y + unit_z * unit_z),
            2.0 * (unit_x * unit_y - unit_w * unit_z),
            2.0 * (unit_x * unit_z + unit_w * unit_y),
        ),
        (
            2.0 * (unit_x * unit_y + unit_w * unit_z),
            1.0 - 2.0 * (unit_x * unit_x + unit_z * unit_z),
            2.0 * (unit_y * unit_z - unit_w * unit_x),
        ),
        (
            2.0 * (unit_x * unit_z - unit_w * unit_y),
            2.0 * (unit_y * unit_z + unit_w * unit_x),
            1.0 - 2.0 * (unit_x * unit_x + unit_y * unit_y),
        ),
    )


def sh_terms(dir_x, dir_y, dir_z):
    sq_x = dir_x * dir_x
    sq_y = dir_y * dir_y
    sq_z = dir_z * dir_z
    return (
        -sh_one * dir_y,
        sh_one * dir_z,
        -sh_one * dir_x,
        sh_two[0] * dir_x * dir_y,
        sh_two[1] * dir_y * dir_z,
        sh_two[2] * (2.0 * sq_z - sq_x - sq_y),
        sh_two[3] * dir_x * dir_z,
        sh_two[4] * (sq_x - sq_y),
        sh_three[0] * dir_y * (3.0 * sq_x - sq_y),
        sh_three[1] * dir_x * dir_y * dir_z,
        sh_three[2] * dir_y * (4.0 * sq_z - sq_x - sq_y),
        sh_three[3] * dir_z * (2.0 * sq_z - 3.0 * sq_x - 3.0 * sq_y),
        sh_three[4] * dir_x * (4.0 * sq_z - sq_x - sq_y),
        sh_three[5] * dir_z * (sq_x - sq_y),
        sh_three[6] * dir_x * (sq_x - 3.0 * sq_y),
    )


def camera_of(cam_ref):
    first = iota((8, 128), 0) < 4
    vals = [jnp.where(first, cam_ref[0, 0, i], cam_ref[0, 1, i]) for i in range(8)]
    rot = rotation(vals[0], vals[1], vals[2], vals[3])
    shift = vals[4:7]
    eye = [-(rot[0][c] * shift[0] + rot[1][c] * shift[1] + rot[2][c] * shift[2]) for c in range(3)]
    return rot, shift, vals[7], eye


def geometry(centre, log_scales, quat, cam):
    cam_rot, shift, focal, _ = cam
    in_cam = [
        cam_rot[r][0] * centre[0] + cam_rot[r][1] * centre[1] + cam_rot[r][2] * centre[2] + shift[r]
        for r in range(3)
    ]
    inv_depth = 1.0 / in_cam[2]
    scaled = focal * inv_depth
    ratio_x = in_cam[0] * inv_depth
    ratio_y = in_cam[1] * inv_depth
    mean_x = focal * ratio_x
    mean_y = focal * ratio_y
    screen_map = [
        [scaled * (cam_rot[0][c] - ratio_x * cam_rot[2][c]) for c in range(3)],
        [scaled * (cam_rot[1][c] - ratio_y * cam_rot[2][c]) for c in range(3)],
    ]
    local_rot = rotation(*quat)
    scales = [jnp.exp(s) for s in log_scales]
    axes = [
        [
            (
                screen_map[r][0] * local_rot[0][c]
                + screen_map[r][1] * local_rot[1][c]
                + screen_map[r][2] * local_rot[2][c]
            )
            * scales[c]
            for c in range(3)
        ]
        for r in range(2)
    ]
    cov_xx = axes[0][0] * axes[0][0] + axes[0][1] * axes[0][1] + axes[0][2] * axes[0][2] + blur_var
    cov_xy = axes[0][0] * axes[1][0] + axes[0][1] * axes[1][1] + axes[0][2] * axes[1][2]
    cov_yy = axes[1][0] * axes[1][0] + axes[1][1] * axes[1][1] + axes[1][2] * axes[1][2] + blur_var
    return mean_x, mean_y, cov_xx, cov_xy, cov_yy


def colours_of(centre, coeffs, cam):
    eye = cam[3]
    view = [centre[c] - eye[c] for c in range(3)]
    inverse = lax.rsqrt(view[0] * view[0] + view[1] * view[1] + view[2] * view[2])
    terms = sh_terms(view[0] * inverse, view[1] * inverse, view[2] * inverse)
    out = []
    for ch in range(3):
        total = sh_zero * coeffs[ch] + 0.5
        for q in range(15):
            total = total + terms[q] * coeffs[3 * (q + 1) + ch]
        out.append(total)
    return out


def precision_of(cov_xx, cov_xy, cov_yy):
    inverse = 1.0 / (cov_xx * cov_yy - cov_xy * cov_xy)
    return cov_yy * inverse, -cov_xy * inverse, cov_xx * inverse


def spread(x_ref, wide):
    for a in range(0, PARAMS, 8):
        n = min(8, PARAMS - a)
        for k in range(4):
            piece = x_ref[a : a + n, 128 * k : 128 * (k + 1)]
            for v in range(2):
                wide[pl.ds(8 * a + 4 * v + k, n, stride=8), :] = piece


def wide_row(wide, i):
    return wide[8 * i : 8 * i + 8, :]


def make_features(wide, cam, centre_y, feat):
    centre = [wide_row(wide, i) for i in range(3)]
    geo = geometry(
        centre, [wide_row(wide, 3 + i) for i in range(3)], [wide_row(wide, 6 + i) for i in range(4)], cam
    )
    prec = precision_of(geo[2], geo[3], geo[4])
    cols = colours_of(centre, [wide_row(wide, 11 + i) for i in range(48)], cam)
    opac = opacity_cap * jax.nn.sigmoid(wide_row(wide, 10))
    values = (*cols, geo[0] + 64.0, geo[1] + centre_y, *prec, opac)
    for f in range(FEATS):
        feat[8 * f : 8 * f + 8, :] = values[f]


def pick_features(sources, opac, index_row):
    row = iota((8, 128), 0)
    first = iota((8, 128), 1) < 64
    index = jnp.broadcast_to(jnp.maximum(index_row, 0), (8, 128))
    low = index & 127
    part = index >> 7
    both = []
    for v in range(2):
        got = [lane_gather(sources[v][k], low) for k in range(4)]
        both.append(
            jnp.where(part < 2, jnp.where(part == 0, got[0], got[1]), jnp.where(part == 2, got[2], got[3]))
        )
    last = jnp.where(row == jnp.where(first, 0, 4) + part, lane_gather(opac, low), 0.0)
    return jnp.where(first, both[0], both[1]), jnp.sum(last, axis=0, keepdims=True)


def sources_of(load):
    return [[load(pl.ds(4 * v + k, 8, stride=8)) for k in range(4)] for v in range(2)]


def lists_kernel(lists_ref, before_ref, live_ref, req_ref):
    sub = iota((SLOTS, SLOTS), 0)
    lane = iota((SLOTS, SLOTS), 1)
    upto = jnp.where(sub <= lane, 1.0, 0.0).astype(bf16)
    number = (iota((SLOTS, 128), 0) + 1).astype(f32).astype(bf16)
    slot = iota((1, SLOTS), 1)
    row8 = iota((8, SLOTS), 0)
    owners = iota((TILES, SLOTS), 0)
    row = iota((8, 128), 0)
    col = iota((8, 128), 1)
    pick = row * CAP + (col & (CAP - 1))
    acc = [jnp.full((8, 128), -1, i32) for _ in range(2)]

    def one(l):
        ids = lists_ref[0, l : l + 1, :]
        live = ids >= 0
        owner = jnp.where(live, ids >> 9, -1)
        local = ids & (SPL - 1)
        mine = owner == owners
        counts = dot(jnp.where(mine, 1.0, 0.0).astype(bf16), upto)
        yield
        rank = jnp.sum(jnp.where(mine, counts, 0.0), axis=0, keepdims=True).astype(i32) - 1
        place = jnp.where(live, owner * CAP + rank, -1)
        chosen = jnp.where(place == sub, 1.0, 0.0).astype(bf16)
        yield
        rows = jnp.where(
            row8 == 0, slot + 1, jnp.where(row8 == 1, local & 255, jnp.where(row8 == 2, local >> 8, 0))
        )
        found = dot_t(rows.astype(f32).astype(bf16), chosen)
        column = dot(chosen, number)
        yield
        order = found[0:1, :]
        before_ref[l] = jnp.where(jnp.concatenate([column, column], axis=1) < order, 1.0, 0.0).astype(bf16)
        yield
        held = order > 0.5
        live_ref[l : l + 1, :] = jnp.where(held, 1.0, 0.0)
        wanted = jnp.where(held, found[1:2, :] + 256.0 * found[2:3, :], -1.0).astype(i32)
        for h in range(2):
            half = jnp.broadcast_to(wanted[:, 128 * h : 128 * (h + 1)], (8, 128))
            acc[h] = jnp.where((col >> 4) == l, lane_gather(half, pick), acc[h])
        yield

    pending = [one(l) for l in range(LISTS)]
    active = []
    while pending or active:
        if pending:
            active.append(pending.pop(0))
        active = [stream for stream in active if next(stream, active) is None]
    for o in range(TILES):
        req_ref[o] = acc[o // 8][o % 8 : o % 8 + 1, :]


def features_kernel(centre_y, x_ref, cam_ref, after_ref, feat_ref, wide):
    spread(x_ref, wide)
    make_features(wide, camera_of(cam_ref), centre_y, feat_ref)


def render_kernel(
    first_round,
    tile_ref,
    msg_in,
    before_ref,
    live_ref,
    goal_ref,
    *rest,
):
    if first_round:
        req_ref, out_ref, msg_ref = rest[0], rest[1], rest[-1]
        rest = rest[2:-1]
        for o in range(TILES):
            main, last = pick_features(
                sources_of(lambda rows: msg_in[o, rows, :]), msg_in[o, 64:72, :], req_ref[o]
            )
            msg_ref[ROWS * o : ROWS * o + 8, :] = main
            msg_ref[ROWS * o + 8 : ROWS * o + 9, :] = last
            out_ref[10 * o + 9 : 10 * o + 10, :] = req_ref[o].astype(f32)
    else:
        msg_ref, out_ref = msg_in, rest[0]
        rest = rest[1:]
    rows_in = ROWS if first_round else FEATS
    rows_out = FEATS + first_round
    feat, grad, grad8, goal8, alpha, lk_h, lk_l, wgt, wgt_h, wgt_l, u_f, u_h, u_l = rest
    row = iota((8, 128), 0)
    col = iota((8, 128), 1)
    block = col >> 4
    inner = col & (CAP - 1)
    for h in range(2):
        starts = [rows_in * (8 * h + o) for o in range(8)]
        whole = [msg_ref[at : at + 8, :] for at in starts]
        ninth = jnp.concatenate([msg_ref[at + 8 : at + 9, :] for at in starts], axis=0)
        for l in range(LISTS):
            got = whole[l]
            for o in range(8):
                if o != l:
                    got = jnp.where(block == o, pltpu.roll(whole[o], (o - l) * CAP % 128, 1), got)
            feat[l, 0:8, 128 * h : 128 * (h + 1)] = got
            last = jnp.where(row == block, lane_gather(ninth, inner + CAP * l), 0.0)
            feat[l, 8:9, 128 * h : 128 * (h + 1)] = jnp.sum(last, axis=0, keepdims=True)
    goal8[...] = jnp.zeros_like(goal8)
    tile = tile_ref[0]
    sub16 = iota((16, SLOTS), 0).astype(f32)
    row8 = iota((8, SLOTS), 0)
    half = -0.5 * log2e
    down = functools.partial(jnp.sum, axis=0, keepdims=True)
    state = [None] * LISTS

    def front(l):
        b = l % BUFS
        number = tile * SCREENS + l % SCREENS
        start_x = (16 * lax.rem(number, 8)).astype(f32) + 0.5
        start_y = (16 * lax.div(number, 8)).astype(f32) + 0.5
        f8 = feat[l, 0:8, :]
        opac = feat[l, 8:9, :] * live_ref[l : l + 1, :]
        off_x = (sub16 + start_x) - f8[3:4, :]
        quad_a = (half * f8[5:6, :]) * off_x * off_x
        quad_b = (2.0 * half * f8[6:7, :]) * off_x
        prec_y = half * f8[7:8, :]
        mean_y = f8[4:5, :]
        state[l] = (f8, off_x, start_y, mean_y)
        for at in range(0, SLOTS, CHUNK):
            for y in range(at // 16, (at + CHUNK) // 16):
                rows = slice(16 * y, 16 * y + 16)
                off_y = (start_y + float(y)) - mean_y
                quad = quad_a + (off_y * quad_b + prec_y * off_y * off_y)
                a = opac * jnp.exp2(quad)
                high, low = split(jnp.log(1.0 - a))
                alpha[b, rows, :] = a
                lk_h[b, rows, :] = high
                lk_l[b, rows, :] = low
                if y % 4 == 3:
                    yield
            rows = slice(at, at + CHUNK)
            before = before_ref[l]
            total = dot(lk_h[b, rows, :], before) + dot(lk_l[b, rows, :], before)
            for sub in range(0, CHUNK, 32):
                rows = slice(at + sub, at + sub + 32)
                w = jnp.exp2(total[sub : sub + 32] * log2e) * alpha[b, rows, :]
                high, low = split(w)
                wgt[b, rows, :] = w
                wgt_h[b, rows, :] = high
                wgt_l[b, rows, :] = low
            yield

    def back(l):
        b = l % BUFS
        f8, off_x, start_y, mean_y = state[l]
        c_h, c_l = split(f8)
        c_hf = c_h.astype(f32)
        c_lf = c_l.astype(f32)
        c_both = jnp.concatenate([c_hf, c_lf], axis=0).astype(bf16)
        image = dot_t(c_both, wgt_h[b])
        image = image[0:8] + (image[8:16] + dot_t(c_h, wgt_l[b]))
        yield
        for ch in range(3):
            goal8[b, ch : ch + 1, :] = goal_ref[0, ch, l : l + 1, :]
        diff = jnp.where(row8 < 3, image - goal8[b], 0.0)
        d_h, d_l = split(diff)
        d_hf = d_h.astype(f32)
        d_lf = d_l.astype(f32)
        d_both = jnp.concatenate([d_hf, d_lf], axis=0).astype(bf16)
        left = jnp.transpose(jnp.concatenate([d_hf, d_hf, d_lf, d_lf], axis=0)).astype(bf16)
        right = jnp.concatenate([c_hf, c_lf, c_hf, c_lf], axis=0).astype(bf16)
        yield
        sums = [jnp.zeros((16, SLOTS), f32) for _ in range(3)]
        before = before_ref[l]
        for at in range(0, SLOTS, CHUNK):
            slopes = dot(left[at : at + CHUNK], right)
            for sub in range(0, CHUNK, 32):
                rows = slice(at + sub, at + sub + 32)
                u = wgt[b, rows, :] * slopes[sub : sub + 32]
                high, low = split(u)
                u_f[b, rows, :] = u
                u_h[b, rows, :] = high
                u_l[b, rows, :] = low
            yield
            rows = slice(at, at + CHUNK)
            later = dot_t(u_h[b, rows, :], before) + dot_t(u_l[b, rows, :], before)
            for sub in range(0, CHUNK, 16):
                rows = slice(at + sub, at + sub + 16)
                a = alpha[b, rows, :]
                part = u_f[b, rows, :] - later[sub : sub + 16] * (a / (1.0 - a))
                off_y = (start_y + float((at + sub) // 16)) - mean_y
                moved = off_y * part
                sums[0] = sums[0] + part
                sums[1] = sums[1] + moved
                sums[2] = sums[2] + off_y * moved
                if sub % 64 == 48:
                    yield
        colour = dot(d_both, wgt_h[b])
        colour = colour[0:8] + (colour[8:16] + dot(d_h, wgt_l[b]))
        by_x = sums[0] * off_x
        moments = (
            down(sums[0]),
            down(by_x),
            down(sums[1]),
            down(by_x * off_x),
            down(sums[1] * off_x),
        )
        for i in range(5):
            colour = jnp.where(row8 == 3 + i, moments[i], colour)
        grad[l] = colour
        grad8[l : l + 1, :] = down(sums[2])
        yield

    for l in range(LISTS + 1):
        streams = ([back(l - 1)] if l > 0 else []) + ([front(l)] if l < LISTS else [])
        while streams:
            streams = [stream for stream in streams if next(stream, streams) is None]

    for h in range(2):
        lanes = slice(128 * h, 128 * (h + 1))
        whole = [grad[l, :, lanes] for l in range(LISTS)]
        ninth = grad8[:, lanes]
        for o in range(8):
            got = whole[o]
            for l in range(LISTS):
                if l != o:
                    got = jnp.where(block == l, pltpu.roll(whole[l], (l - o) * CAP % 128, 1), got)
            at = rows_out * (8 * h + o)
            out_ref[at : at + 8, :] = got
            last = jnp.where(row == block, lane_gather(ninth, inner + CAP * o), 0.0)
            out_ref[at + 8 : at + 9, :] = jnp.sum(last, axis=0, keepdims=True)


def hits_of(hits, wanted, t, sub_n):
    hits[:, 128 * t : 128 * (t + 1)] = jnp.where(wanted == sub_n, 1.0, 0.0).astype(bf16)


def prox_kernel(first_round, w_ref, bidx_ref, *rest):
    if first_round:
        x_ref, z_ref, u_ref, add_ref, inv_ref, prox, pad = rest
        pad[0:PARAMS, :] = x_ref[...]
        sub_n = iota((SPL, NB), 0)
        lane = iota((8, NB), 1)
        total = jnp.zeros((8, SPL), f32)
        for e in range(2):
            hit = jnp.where(bidx_ref[0, e : e + 1, :] == sub_n, 1.0, 0.0).astype(bf16)
            total = total + dot_t((lane + (NB * e + 1)).astype(f32).astype(bf16), hit)
        inv_ref[...] = total.astype(i32) - 1
    else:
        inv_ref, req_ref, side_ref, near_ref, far_ref, u_ref, add_ref, dual_ref, hits_ref, prox = rest
        partner = partners(w_ref, near_ref, far_ref)
        sub_n = iota((SPL, 128), 0)
        for t in range(TILES):
            hits_of(hits_ref, req_ref[t], t, sub_n)
    for e in range(2):
        w = w_ref[e]
        if first_round:
            for a in range(0, PARAMS, 8):
                n = min(8, PARAMS - a)
                mine = side_columns(pad, bidx_ref, a, e)[0:n]
                prox[a : a + n, NB * e : NB * (e + 1)] = (penalty * w) * (
                    mine - z_ref[0, e, a : a + n, :] + u_ref[0, e, a : a + n, :]
                )
        else:
            agreed, dual = settle(w, side_ref[e], u_ref[0, e], partner[e])
            dual_ref[0, e] = dual
            prox[0:PARAMS, NB * e : NB * (e + 1)] = (penalty * w) * (side_ref[e] - agreed + dual)
    for a in range(0, PARAMS, 8):
        n = min(8, PARAMS - a)
        for k in range(4):
            lanes = slice(128 * k, 128 * (k + 1))
            inverse = inv_ref[:, lanes]
            low = inverse & 127
            add = jnp.where(
                inverse < 128,
                lane_gather(prox[a : a + 8, 0:128], low),
                lane_gather(prox[a : a + 8, 128:256], low),
            )
            add_ref[a : a + n, lanes] = jnp.where(inverse >= 0, add, 0.0)[0:n]


def side_columns(x_ref, bidx_ref, a, e):
    index = jnp.broadcast_to(bidx_ref[0, e : e + 1, :], (8, NB))
    low = index & 127
    part = index >> 7
    got = [lane_gather(x_ref[a : a + 8, 128 * k : 128 * (k + 1)], low) for k in range(4)]
    return jnp.where(
        part < 2, jnp.where(part == 0, got[0], got[1]), jnp.where(part == 2, got[2], got[3])
    )


def adam(step, g, x, m, v):
    m = beta_one * m + (1.0 - beta_one) * g
    v = beta_two * v + (1.0 - beta_two) * g * g
    corr_one = 1.0 - beta_one**step
    corr_two = 1.0 - beta_two**step
    x = x - (learn_rate / corr_one) * m / (jnp.sqrt(v * (1.0 / corr_two)) + adam_eps)
    return x, m, v


def adam_kernel(step, g_ref, x_ref, m_ref, v_ref, xo_ref, mo_ref, vo_ref):
    xo_ref[...], mo_ref[...], vo_ref[...] = adam(step, g_ref[...], x_ref[...], m_ref[...], v_ref[...])


def update_kernel(
    step,
    last_round,
    centre_y,
    w_ref,
    cam_ref,
    gmsg_ref,
    *rest,
):
    if last_round:
        hits, *rest = rest
    (x_ref, m_ref, v_ref, bidx_ref, add_ref, u_ref), rest = rest[:6], rest[6:]
    if last_round:
        g_ref, *rest = rest
    else:
        (xo_ref, mo_ref, vo_ref), rest = rest[:3], rest[3:]
    (side_ref, near_ref, far_ref), rest = rest[:3], rest[3:]
    if last_round:
        wide, gin, gwide, terms, pad, grad = rest
    else:
        msg_ref, req_out, wide, feat, gin, gwide, terms, hits, pad, grad = rest
    rows_in = FEATS if last_round else FEATS + 1
    first = iota((ROWS, 128), 1) < 64
    sub_n = iota((SPL, 128), 0)
    for t in range(TILES):
        lanes = slice(128 * t, 128 * (t + 1))
        at = rows_in * t
        ninth = jnp.broadcast_to(gmsg_ref[at + 8 : at + 9, :], (8, 128))
        high, low = split(jnp.concatenate([gmsg_ref[at : at + 8, :], ninth], axis=0))
        zero = jnp.zeros_like(high)
        terms[0:16, lanes] = jnp.where(first, high, zero)
        terms[16:32, lanes] = jnp.where(first, zero, high)
        terms[32:48, lanes] = jnp.where(first, low, zero)
        terms[48:64, lanes] = jnp.where(first, zero, low)
        if not last_round:
            wanted = gmsg_ref[at + 9 : at + 10, :].astype(i32)
            req_out[t] = wanted
            hits_of(hits, wanted, t, sub_n)
    found = dot_t(terms[...], hits[...])
    total = found[0:32, :] + found[32:64, :]
    for v in range(2):
        for k in range(4):
            lanes = slice(128 * k, 128 * (k + 1))
            gin[pl.ds(4 * v + k, 8, stride=8), :] = total[16 * v : 16 * v + 8, lanes]
            gin[64 + 4 * v + k : 65 + 4 * v + k, :] = total[16 * v + 8 : 16 * v + 9, lanes]
    got = [gin[8 * f : 8 * f + 8, :] for f in range(FEATS)]

    spread(x_ref, wide)
    cam = camera_of(cam_ref)
    centre = [wide_row(wide, i) for i in range(3)]
    log_scales = [wide_row(wide, 3 + i) for i in range(3)]
    quat = [wide_row(wide, 6 + i) for i in range(4)]
    coeffs = [wide_row(wide, 11 + i) for i in range(48)]
    geo, geo_back = jax.vjp(lambda a, b, c: geometry(a, b, c, cam), centre, log_scales, quat)
    p_xx, p_xy, p_yy = precision_of(geo[2], geo[3], geo[4])
    h_sum, m_x, m_y, m_xx, m_xy, m_yy = got[3:9]
    a_xx = p_xx * m_xx + p_xy * m_xy
    a_xy = p_xx * m_xy + p_xy * m_yy
    a_yx = p_xy * m_xx + p_yy * m_xy
    a_yy = p_xy * m_xy + p_yy * m_yy
    geo_grad = (
        p_xx * m_x + p_xy * m_y,
        p_xy * m_x + p_yy * m_y,
        0.5 * (a_xx * p_xx + a_xy * p_xy),
        a_xx * p_xy + a_xy * p_yy,
        0.5 * (a_yx * p_xy + a_yy * p_yy),
    )
    g_centre, g_scales, g_quat = geo_back(geo_grad)
    _, col_back = jax.vjp(lambda a, b: colours_of(a, b, cam), centre, coeffs)
    g_centre2, g_coeffs = col_back(list(got[0:3]))
    g_opac = h_sum * (1.0 - jax.nn.sigmoid(wide_row(wide, 10)))
    grads = (
        [g_centre[i] + g_centre2[i] for i in range(3)] + list(g_scales) + list(g_quat) + [g_opac] + list(g_coeffs)
    )
    for i in range(PARAMS):
        gwide[8 * i : 8 * i + 8, :] = grads[i]

    for a in range(0, PARAMS, 8):
        n = min(8, PARAMS - a)
        for k in range(4):
            lanes = slice(128 * k, 128 * (k + 1))
            both = gwide[pl.ds(8 * a + k, 8, stride=8), :] + gwide[pl.ds(8 * a + 4 + k, 8, stride=8), :]
            grad[a : a + n, lanes] = both[0:n] + add_ref[a : a + n, lanes]
    x, m, v = adam(step, grad[0:PARAMS, :], x_ref[...], m_ref[...], v_ref[...])
    if last_round:
        g_ref[...] = grad[0:PARAMS, :]
    else:
        xo_ref[...] = x
        mo_ref[...] = m
        vo_ref[...] = v
    pad[0:PARAMS, :] = x
    even = w_ref[2] > 0.5
    for a in range(0, PARAMS, 8):
        n = min(8, PARAMS - a)
        shared = []
        for e in range(2):
            mine = side_columns(pad, bidx_ref, a, e)[0:n]
            side_ref[e, a : a + n, :] = mine
            shared.append(mine + u_ref[0, e, a : a + n, :])
        near_ref[a : a + n, :] = jnp.where(even, shared[1], shared[0])
        far_ref[a : a + n, :] = jnp.where(even, shared[0], shared[1])
    if not last_round:
        spread(pad, wide)
        make_features(wide, cam, centre_y, feat)
        sources = sources_of(lambda rows: feat[rows, :])
        opac = feat[64:72, :]
        for t in range(TILES):
            main, last = pick_features(
                sources, opac, gmsg_ref[rows_in * t + 9 : rows_in * t + 10, :].astype(i32)
            )
            msg_ref[FEATS * t : FEATS * t + 8, :] = main
            msg_ref[FEATS * t + 8 : FEATS * t + 9, :] = last


def partners(w_ref, near_ref, far_ref):
    even = w_ref[2] > 0.5
    near = near_ref[...]
    far = far_ref[...]
    return jnp.where(even, far, near), jnp.where(even, near, far)


def settle(w, own, dual, partner):
    agreed = w * (own + dual + partner) * 0.5 + (1.0 - w) * own
    return agreed, dual + w * (own - agreed)


def consensus_kernel(w_ref, side_ref, u_ref, near_ref, far_ref, zo_ref, uo_ref):
    partner = partners(w_ref, near_ref, far_ref)
    for e in range(2):
        agreed, dual = settle(w_ref[e], side_ref[e], u_ref[0, e], partner[e])
        zo_ref[:, e, :] = agreed
        uo_ref[:, e, :] = dual


def shape(dims, kind=f32):
    return jax.ShapeDtypeStruct(dims, kind)


def on_device(
    params, moment1, moment2, tile_lists, cameras, targets, boundary_index, links, consensus, duals
):
    block_total = lax.axis_size("block")
    tile_idx = lax.axis_index("tile")
    block_idx = lax.axis_index("block")
    centre_y = 8.0 * (TILES * SCREENS // 8)
    link_vals = links.astype(f32)
    right_w = jnp.where(block_idx < block_total - 1, link_vals[block_idx], 0.0)
    left_w = jnp.where(block_idx > 0, link_vals[jnp.maximum(block_idx - 1, 0)], 0.0)
    even = block_idx % 2 == 0
    side_w = jnp.stack([left_w, right_w, jnp.where(even, 1.0, 0.0)])
    goals = jnp.transpose(targets, (0, 2, 1, 3))
    tile_num = tile_idx.astype(i32).reshape(1)

    def call(kernel, name, outs, ins, scratch=()):
        return pl.pallas_call(
            kernel,
            out_shape=outs,
            in_specs=ins,
            out_specs=jax.tree.map(lambda _: ANY_VMEM, outs),
            scratch_shapes=list(scratch),
            compiler_params=pltpu.CompilerParams(vmem_limit_bytes=GRANT),
            cost_estimate=pl.CostEstimate(
                flops=MICROS[name] * 10**9, bytes_accessed=MICROS[name] * 3 * 10**6, transcendentals=0
            ),
        )

    wide_scratch = VMEM((512, 128), f32)
    before, live, wanted = call(
        lists_kernel,
        "lists",
        (shape((LISTS, SLOTS, SLOTS), bf16), shape((LISTS, SLOTS)), shape((TILES, 1, 128), i32)),
        [ANY_VMEM],
    )(tile_lists)
    features = call(
        functools.partial(features_kernel, centre_y),
        "features",
        shape((WIDE, 128)),
        [ANY_VMEM, ANY_SMEM, ANY_VMEM],
        [wide_scratch],
    )(params, cameras, live)
    message = lax.all_gather(features, "tile")

    def exchange(value, rows):
        moved = lax.all_to_all(value.reshape(TILES, 1, rows * 128), "tile", 0, 0, tiled=True)
        return moved.reshape(TILES * rows, 128)

    def render(first_round):
        scratch = [
            VMEM((LISTS, 16, SLOTS), f32),
            VMEM((LISTS, 8, SLOTS), f32),
            VMEM((LISTS, SLOTS), f32),
            VMEM((BUFS, 8, SLOTS), f32),
        ]
        for kind in (f32, bf16, bf16, f32, bf16, bf16, f32, bf16, bf16):
            scratch.append(VMEM((BUFS, SLOTS, SLOTS), kind))
        if first_round:
            scratch.append(VMEM((TILES * ROWS, 128), f32))
        return call(
            functools.partial(render_kernel, first_round),
            "render",
            shape((TILES * (FEATS + first_round), 128)),
            [ANY_SMEM] + [ANY_VMEM] * (5 if first_round else 4),
            scratch,
        )

    def swapped(x, first):
        pairs = [(i, i + 1) for i in range(first, block_total - 1, 2)]
        return lax.ppermute(x, "block", pairs + [(j, i) for i, j in pairs])

    values, moment_one, moment_two = params, moment1, moment2
    dual_vars = duals
    for round_idx in range(ROUNDS):
        last_round = round_idx == ROUNDS - 1
        first_round = round_idx == 0
        if first_round:
            sent = render(True)(tile_num, message, before, live, goals, wanted)
        else:
            received = exchange(message, FEATS)
            sent = render(False)(tile_num, received, before, live, goals)
        back = exchange(sent, FEATS + first_round)
        dense = shape((PARAMS, SPL))
        prox_scratch = [VMEM((64, 2 * NB), f32)]
        if first_round:
            add, inverse = call(
                functools.partial(prox_kernel, True),
                "prox",
                (dense, shape((8, SPL), i32)),
                [ANY_SMEM] + [ANY_VMEM] * 4,
                prox_scratch + [VMEM((64, SPL), f32)],
            )(side_w, boundary_index, values, consensus, duals)
            known = ()
        else:
            add, dual_vars, hits = call(
                functools.partial(prox_kernel, False),
                "prox",
                (dense, shape((1, 2, PARAMS, NB)), shape((SPL, TILES * 128), bf16)),
                [ANY_SMEM] + [ANY_VMEM] * 7,
                prox_scratch,
            )(side_w, boundary_index, inverse, requests, own_sides, near, far, dual_vars)
            known = (hits,)
        outs = [dense] * (1 if last_round else 3)
        outs += [shape((2, PARAMS, NB))] + [shape((PARAMS, NB))] * 2
        scratch = [wide_scratch]
        if not last_round:
            outs += [shape((TILES * FEATS, 128)), shape((TILES, 1, 128), i32)]
            scratch += [VMEM((WIDE, 128), f32)]
        scratch += [VMEM((WIDE, 128), f32), VMEM((512, 128), f32), VMEM((64, TILES * 128), bf16)]
        if not last_round:
            scratch += [VMEM((SPL, TILES * 128), bf16)]
        scratch += [VMEM((64, SPL), f32), VMEM((64, SPL), f32)]
        outs = call(
            functools.partial(update_kernel, first_step + round_idx + 1, last_round, centre_y),
            "update",
            tuple(outs),
            [ANY_SMEM, ANY_SMEM] + [ANY_VMEM] * (7 + len(known)),
            scratch,
        )(
            side_w,
            cameras,
            back,
            *known,
            values,
            moment_one,
            moment_two,
            boundary_index,
            add,
            dual_vars,
        )
        if last_round:
            grads, own_sides, near, far = outs
        else:
            *changed, own_sides, near, far, message, requests = outs
        far = swapped(far, 1)
        near = swapped(near, 0)
        if not last_round:
            values, moment_one, moment_two = changed
        else:
            values, moment_one, moment_two = call(
                functools.partial(adam_kernel, first_step + ROUNDS),
                "adam",
                (shape((PARAMS, SPL)),) * 3,
                [ANY_VMEM] * 4,
            )(grads, values, moment_one, moment_two)
            sides = (shape((PARAMS, 2, NB)),) * 2
            sides = call(consensus_kernel, "consensus", sides, [ANY_SMEM] + [ANY_VMEM] * 4)(
                side_w, own_sides, dual_vars, near, far
            )
            agreed, dual_vars = (jnp.transpose(side, (1, 0, 2))[None] for side in sides)
    return (values, moment_one, moment_two, agreed, dual_vars)


def solution(mesh):
    both = ("block", "tile")
    placed = (
        P(None, both),
        P(None, both),
        P(None, both),
        P(both, None, None),
        P("block", None, None),
        P(both, None, None, None),
        P(both, None, None),
        P(),
        P(both, None, None, None),
        P(both, None, None, None),
    )
    return jax.shard_map(
        on_device,
        mesh=mesh,
        in_specs=placed,
        out_specs=(
            P(None, both),
            P(None, both),
            P(None, both),
            P(both, None, None, None),
            P(both, None, None, None),
        ),
        check_vma=False,
    )
```
